256 devices in a mesh: feat: 16 (over z, core), dom: 16 (over x, y).
Axes of the slice: x: 4, y: 4, z: 8, core: 2. Of those that a mesh axis runs over, the one named last changes fastest.
Arguments:
- features: bfloat16 [16, 1024, 9216], P('dom', 'feat'), may hold values from -6 to 6
- w1_self: bfloat16 [1024, 256], P('feat'), may hold values from -0.1875 to 0.1875
- w1_neigh: bfloat16 [1024, 256], P('feat'), may hold values from -0.1875 to 0.1875
- w2_self: bfloat16 [256, 256], replicated, may hold values from -0.375 to 0.375
- w2_neigh: bfloat16 [256, 256], replicated, may hold values from -0.375 to 0.375
- neigh_one: int32 [16, 10, 4608], P('dom'), may hold values from 0 to 9215
- send_rows: int32 [16, 16, 16, 128], P('dom', 'feat'), may hold values from 0 to 287
- recv_count: int32 [16, 16, 16], P(None, 'feat', 'dom'), may hold values from 1 to 128, as said below
- neigh_two: int32 [16, 16, 256, 15], P('dom', 'feat'), may hold values from 0 to 2047, as said below
- seed_rows: int32 [16, 16, 256], P('dom', 'feat'), may hold values from 0 to 287, as said below
- d_out: bfloat16 [16, 16, 256, 256], P('dom', 'feat'), may hold values from -0.0625 to 0.0625
Outputs:
- layer_two: bfloat16 [16, 16, 256, 256], P('dom', 'feat')
- grad_w1_self: float32 [1024, 256], P('feat')
- grad_w1_neigh: float32 [1024, 256], P('feat')
- grad_w2_self: float32 [256, 256], replicated
- grad_w2_neigh: float32 [256, 256], replicated
The draws below stay inside these ranges and needn't reach their ends.
Inputs may be any that keep to these rules, and one draw needn't show every extreme that they name: `neigh_one`: columns of the partition's 9216 input nodes. `send_rows`: rows among the sending device's 288 owned nodes. `recv_count`: the live slots of a buffer are its leading ones; every receiver gets a full buffer of 128 live rows from some source, and some receiver gets full buffers from every source. `neigh_two`: each is below the total of the receiving device's counts; on every device some seed names the last live row. `seed_rows`: distinct within one device.
All inputs are finite; a program needn't handle non-finite values.
Results may differ from the reference program's by a relative error of at most 0.0051.
Values may be sent and summed in bfloat16 or wider, within the bound.
No kernel may reach another device: no remote copies, remote signals or barrier semaphores. Data moves between devices by JAX's collectives and lax.ppermute only.
A program may use at most 64 MiB of HBM per device.

```python
import jax
import jax.numpy as jnp
from jax import lax

IN = 1024
HID = 256
K1 = 10
K2 = 15
OWN = 288
SEEDS = 256
SLOTS = 128
R1 = 4608
NIN = 9216
N_FEAT = 16
N_DOM = 16


def count_table(key):
    base_key = jax.random.fold_in(key, 11)
    heat_key, count_key, full_key, busy_key = jax.random.split(base_key, 4)
    heat = jax.random.randint(heat_key, (1, N_FEAT, N_DOM), 1, 5)
    ceiling = jnp.maximum(SLOTS * heat // 4, 1)
    counts = jax.random.randint(count_key, (N_DOM, N_FEAT, N_DOM), 1, ceiling + 1)
    full_source = jax.random.randint(full_key, (1, N_FEAT, N_DOM), 0, N_DOM)
    source_ids = jnp.arange(N_DOM, dtype=jnp.int32).reshape(N_DOM, 1, 1)
    counts = jnp.where(source_ids == full_source, SLOTS, counts)
    busy = jax.random.randint(busy_key, (), 0, N_FEAT * N_DOM)
    receiver_ids = jnp.arange(N_FEAT, dtype=jnp.int32).reshape(1, N_FEAT, 1) * N_DOM + jnp.arange(N_DOM, dtype=jnp.int32).reshape(1, 1, N_DOM)
    return jnp.where(receiver_ids == busy, SLOTS, counts).astype(jnp.int32)


def draw_recv_count(key, part):
    return count_table(key)


def draw_neigh_two(key, part):
    counts = count_table(key)
    live_rows = jnp.sum(counts, axis=0).T
    ceiling = live_rows[:, :, None, None]
    drawn = jax.random.randint(jax.random.fold_in(key, 23), (N_DOM, N_FEAT, SEEDS, K2), 0, ceiling)
    seed_pick = jax.random.randint(jax.random.fold_in(key, 29), (N_DOM, N_FEAT, 1, 1), 0, SEEDS)
    column_pick = jax.random.randint(jax.random.fold_in(key, 31), (N_DOM, N_FEAT, 1, 1), 0, K2)
    seed_ids = jnp.arange(SEEDS, dtype=jnp.int32).reshape(1, 1, SEEDS, 1)
    column_ids = jnp.arange(K2, dtype=jnp.int32).reshape(1, 1, 1, K2)
    marked = (seed_ids == seed_pick) & (column_ids == column_pick)
    return jnp.where(marked, ceiling - 1, drawn).astype(jnp.int32)


def draw_seed_rows(key, part):
    scores = jax.random.randint(jax.random.fold_in(key, 37), (N_DOM, N_FEAT, OWN), 0, 2 ** 20)
    scores = scores * OWN + jnp.arange(OWN, dtype=jnp.int32)
    order = jnp.argsort(scores, axis=-1)
    return order[:, :, :SEEDS].astype(jnp.int32)


def touch_ends(values, stream_key, low, top_value):
    shape = values.shape
    spot = [jax.random.randint(jax.random.fold_in(stream_key, axis), (), 0, shape[axis]) for axis in range(len(shape))]
    values = values.at[tuple(spot)].set(low)
    longest = shape.index(max(shape))
    spot[longest] = (spot[longest] + 1) % shape[longest]
    return values.at[tuple(spot)].set(top_value)


def block_levels(own_key, shape, cuts, least, largest):
    def one(dim, blocks):
        steps = jax.random.uniform(jax.random.fold_in(jax.random.fold_in(own_key, 6), dim), (blocks,), jnp.float32, least / len(cuts), largest / len(cuts))
        return jnp.repeat(jnp.exp(steps), shape[dim] // blocks).reshape((-1,) + (1,) * (len(shape) - dim - 1))

    loudness = one(*cuts[0])
    for cut in cuts[1:]:
        loudness = loudness * one(*cut)
    return loudness


def scatter_about(stream_key, shape, scale, most, pieces=(), kind=jnp.bfloat16):
    gain = block_levels(stream_key, shape, pieces, -0.22, 0.18) if pieces else 1.0
    result = jax.random.normal(stream_key, shape, jnp.float32) * scale * gain
    return jnp.minimum(jnp.maximum(result, -most), most).astype(kind)


def setup_inputs(seed: int = 0) -> dict:
    key_list = jax.random.split(jax.random.key(seed), 12)
    features = scatter_about(key_list[0], (N_DOM, IN, NIN), 1.0, 6.0, ((0, 16), (1, 16)))
    w1_self = scatter_about(key_list[1], (IN, HID), IN ** -0.5, 0.1875, ((0, 16),))
    w1_neigh = scatter_about(key_list[2], (IN, HID), IN ** -0.5, 0.1875, ((0, 16),))
    w2_self = scatter_about(key_list[3], (HID, HID), HID ** -0.5, 0.375)
    w2_neigh = scatter_about(key_list[4], (HID, HID), HID ** -0.5, 0.375)
    neigh_one = touch_ends(jax.random.randint(key_list[5], (N_DOM, K1, R1), 0, NIN), jax.random.fold_in(key_list[5], 1), 0, NIN - 1).astype(jnp.int32)
    send_rows = touch_ends(jax.random.randint(key_list[6], (N_DOM, N_FEAT, N_DOM, SLOTS), 0, OWN), jax.random.fold_in(key_list[6], 1), 0, OWN - 1).astype(jnp.int32)
    recv_count = draw_recv_count(jax.random.fold_in(key_list[11], 71), 0)
    neigh_two = draw_neigh_two(jax.random.fold_in(key_list[11], 71), 0)
    seed_rows = draw_seed_rows(jax.random.fold_in(key_list[11], 71), 0)
    d_out = scatter_about(key_list[10], (N_DOM, N_FEAT, SEEDS, HID), ((SEEDS * N_FEAT * N_DOM) ** -0.5), 0.0625, ((0, 16), (1, 16)))
    return {"features": features, "w1_self": w1_self, "w1_neigh": w1_neigh, "w2_self": w2_self, "w2_neigh": w2_neigh, "neigh_one": neigh_one, "send_rows": send_rows, "recv_count": recv_count, "neigh_two": neigh_two, "seed_rows": seed_rows, "d_out": d_out}


def reference(features, w1_self, w1_neigh, w2_self, w2_neigh, neigh_one, send_rows, recv_count, neigh_two, seed_rows, d_out):
    def first_layer(inputs):
        feature_table, neigh_lists = inputs
        running = jnp.zeros((IN, R1), jnp.float32)
        for column in range(K1):
            running = running + jnp.take(feature_table, neigh_lists[column], axis=1).astype(jnp.float32)
        mean_cols = (running / K1).astype(jnp.bfloat16)
        dims = (((0,), (0,)), ((), ()))
        pre_rows = lax.dot_general(feature_table[:, :R1], w1_self, dims, preferred_element_type=jnp.float32) + lax.dot_general(mean_cols, w1_neigh, dims, preferred_element_type=jnp.float32)
        return mean_cols, pre_rows

    mean_one, pre_one = lax.map(first_layer, (features, neigh_one))
    hidden = jax.nn.elu(pre_one).astype(jnp.bfloat16).reshape(N_DOM, N_FEAT, OWN, HID)

    def send_list(hidden_rows, index_rows):
        return jnp.take(hidden_rows, index_rows.reshape(-1), axis=0).reshape(N_DOM, SLOTS, HID)

    outgoing = jax.vmap(jax.vmap(send_list))(hidden, send_rows)
    incoming = outgoing.transpose(2, 1, 0, 3, 4).reshape(N_DOM, N_FEAT, N_DOM * SLOTS, HID)
    counts = recv_count.transpose(2, 1, 0)
    starts = jnp.cumsum(counts, axis=2) - counts
    source = jnp.sum((neigh_two[..., None] >= starts[:, :, None, None, 1:]).astype(jnp.int32), axis=-1)
    picked = (source[..., None] == jnp.arange(N_DOM, dtype=jnp.int32)).astype(jnp.int32)
    offset_of = jnp.sum(picked * starts[:, :, None, None, :], axis=-1)
    where_in = (source * SLOTS + neigh_two - offset_of).astype(jnp.int32)

    def second_layer(flat_in, positions, hidden_rows, seeds, grad_out):
        running = jnp.zeros((SEEDS, HID), jnp.float32)
        for column in range(K2):
            running = running + jnp.take(flat_in, positions[:, column], axis=0).astype(jnp.float32)
        mean_two = (running / K2).astype(jnp.bfloat16)
        self_two = jnp.take(hidden_rows, seeds, axis=0)
        layer_out = (jnp.dot(self_two, w2_self, preferred_element_type=jnp.float32) + jnp.dot(mean_two, w2_neigh, preferred_element_type=jnp.float32)).astype(jnp.bfloat16)
        d_self = jnp.dot(grad_out, w2_self.T, preferred_element_type=jnp.float32)
        d_mean = jnp.dot(grad_out, w2_neigh.T, preferred_element_type=jnp.float32) / K2
        slot_sum = jnp.zeros((N_DOM * SLOTS, HID), jnp.float32)
        for column in range(K2):
            slot_sum = slot_sum.at[positions[:, column]].add(d_mean)
        return layer_out, self_two, mean_two, d_self, slot_sum.astype(jnp.bfloat16)

    layer_two, self_two, mean_two, d_self, slot_grad = jax.vmap(jax.vmap(second_layer))(incoming, where_in, hidden, seed_rows, d_out)
    grad_out32 = d_out.astype(jnp.float32)
    grad_w2_self = jnp.einsum("qfih,qfio->ho", self_two.astype(jnp.float32), grad_out32, precision=lax.Precision.HIGHEST)
    grad_w2_neigh = jnp.einsum("qfih,qfio->ho", mean_two.astype(jnp.float32), grad_out32, precision=lax.Precision.HIGHEST)
    returned = slot_grad.reshape(N_DOM, N_FEAT, N_DOM, SLOTS, HID).transpose(2, 1, 0, 3, 4)

    def owner_grads(back_rows, index_rows, seeds, self_grads):
        d_hidden = jnp.zeros((OWN, HID), jnp.float32)
        d_hidden = d_hidden.at[index_rows.reshape(-1)].add(back_rows.reshape(-1, HID).astype(jnp.float32))
        return d_hidden.at[seeds].add(self_grads)

    d_hidden = jax.vmap(jax.vmap(owner_grads))(returned, send_rows, seed_rows, d_self).reshape(N_DOM, R1, HID)
    elu_slope = jnp.where(pre_one > 0, 1.0, jnp.exp(jnp.minimum(pre_one, 0.0)))
    d_pre = (d_hidden * elu_slope).astype(jnp.bfloat16)

    def accumulate(running, inputs):
        feature_table, mean_cols, grad_rows = inputs
        first_self = running[0] + jnp.dot(feature_table[:, :R1], grad_rows, preferred_element_type=jnp.float32)
        first_mean = running[1] + jnp.dot(mean_cols, grad_rows, preferred_element_type=jnp.float32)
        return (first_self, first_mean), None

    zeros_in = jnp.zeros((IN, HID), jnp.float32)
    (grad_w1_self, grad_w1_neigh), unused = lax.scan(accumulate, (zeros_in, zeros_in), (features, mean_one, d_pre))
    return (layer_two, grad_w1_self, grad_w1_neigh, grad_w2_self, grad_w2_neigh)
```

```python
import jax
import jax.numpy as jnp
from jax import lax
from jax.experimental import pallas as pl
from jax.experimental.pallas import tpu as pltpu
from jax.sharding import PartitionSpec as P

BF = jnp.bfloat16
F32 = jnp.float32
I32 = jnp.int32
NF = 16
ND = 16
NZ = 8
COLS = 64
PAIR = 128
NIN = 9216
R1 = 4608
OWN = 288
HALF = R1 // 2
K1 = 10
K2 = 15
SEEDS = 256
SLOTS = 128
HID = 256
UNROLL = 16
VMEM = pl.BlockSpec(memory_space=pltpu.VMEM)
SMEM = pl.BlockSpec(memory_space=pltpu.SMEM)


def call(body, name, outs, ins, scratch=(), limit=48):
    return pl.pallas_call(
        body,
        name=name,
        out_shape=outs,
        in_specs=ins,
        out_specs=jax.tree.map(lambda _: VMEM, outs),
        scratch_shapes=list(scratch),
        compiler_params=pltpu.CompilerParams(vmem_limit_bytes=limit << 20),
    )


def shape(dims, dtype):
    return jax.ShapeDtypeStruct(dims, dtype)


def dot(a, b, ca=1, cb=0):
    return lax.dot_general(a, b, (((ca,), (cb,)), ((), ())), preferred_element_type=F32)


def pick_body(count_ref, neigh_ref, dout_ref, picks_ref, t_ref):
    start = jnp.int32(0)
    lanes = neigh_ref[...]
    d_out = dout_ref[...]
    row = lax.broadcasted_iota(I32, (SLOTS, SEEDS), 0)
    for s in range(ND):
        count = count_ref[s]
        position = jnp.where(row < count, row + start, -1)
        total = jnp.zeros((SLOTS, SEEDS), F32)
        for k in range(K2):
            total = total + jnp.where(position == lanes[k : k + 1, :], 1.0, 0.0)
        picks = total.astype(BF)
        picks_ref[s] = picks
        t_ref[s] = dot(picks, d_out).astype(BF)
        start = start + count


def fill_table(core, own_ref, other_ref, table, nodes, step=512):
    first = core == 0
    for c in range(0, nodes, step):
        own = own_ref[:, c : c + step].astype(F32)
        other = other_ref[:, c : c + step].astype(F32)
        low = jnp.where(first, own, other)
        high = jnp.where(first, other, own)
        table[c : c + step, :] = jnp.concatenate([low, high], axis=0).T


def self_body(core_ref, own_ref, other_ref, self_ref, table):
    core = core_ref[0]
    fill_table(core, own_ref, other_ref, table, R1)
    for z in range(NZ):
        base = pl.multiple_of((2 * z + core) * OWN, 32)
        self_ref[z] = table[pl.ds(base, OWN), :].astype(BF)


def mean_body(core_ref, own_ref, other_ref, index_ref, mean_ref, table, sums):
    fill_table(core_ref[0], own_ref, other_ref, table, NIN)

    def block(b, carry):
        base = pl.multiple_of(b * UNROLL, UNROLL)
        for j in range(UNROLL):
            rows = [table[pl.ds(index_ref[k * HALF + base + j], 1), :] for k in range(K1)]
            while len(rows) > 1:
                even = len(rows) // 2 * 2
                rows = [rows[i] + rows[i + 1] for i in range(0, even, 2)] + rows[even:]
            sums[pl.ds(base + j, 1), :] = rows[0]
        return carry

    lax.fori_loop(0, HALF // UNROLL, block, 0)
    for z in range(NZ):
        mean_ref[z] = (sums[z * OWN : (z + 1) * OWN, :] * (1.0 / K1)).astype(BF)


def split(x):
    high = x.astype(BF)
    return high, (x - high.astype(F32)).astype(BF)


def owner_body(t_ref, send_ref, seed_ref, dout_ref, w2s_ref, w2n_ref, x_ref, d_ref, dh_ref):
    d_out = dout_ref[...]
    row = lax.broadcasted_iota(I32, (OWN, SEEDS), 0)
    x = jnp.zeros((OWN, HID), F32)
    for q in range(0, ND, 2):
        lanes = jnp.concatenate([send_ref[q : q + 1, :], send_ref[q + 1 : q + 2, :]], axis=1)
        hot = jnp.where(row == lanes, 1.0, 0.0).astype(BF)
        x = x + dot(hot, t_ref[q * SLOTS : (q + 2) * SLOTS, :])
    x = x * (1.0 / K2)
    hot = jnp.where(row == seed_ref[...], 1.0, 0.0).astype(BF)
    d = dot(hot, d_out).astype(BF)
    high, low = split(x)
    w2n = w2n_ref[...]
    x_ref[...] = x
    d_ref[...] = d
    dh_ref[...] = dot(high, w2n, 1, 1) + dot(low, w2n, 1, 1) + dot(d, w2s_ref[...], 1, 1)


def main_body(
    self_ref, mean_ref, w_ref, x_ref, d_ref, dh_ref, send_ref, seed_ref, w2s_ref,
    g1_ref, g2_ref, out_ref, part_ref, w1,
):
    for f in range(NF):
        for q in range(ND):
            r, h = q // 2, q % 2
            base = f * COLS + (r % 4) * 16
            w1[r // 4, base : base + 16, h * 128 : (h + 1) * 128] = w_ref[q, f]
    pre = jnp.zeros((OWN, HID), F32)
    for z in range(NZ):
        pre = pre + dot(self_ref[z], w1[0, z * PAIR : (z + 1) * PAIR, :])
        pre = pre + dot(mean_ref[z], w1[1, z * PAIR : (z + 1) * PAIR, :])
    slope = jnp.exp(jnp.minimum(pre, 0.0))
    hidden = jnp.where(pre > 0, pre, slope - 1.0).astype(BF)
    d_pre = (dh_ref[...] * slope).astype(BF)
    for z in range(NZ):
        gs = dot(self_ref[z], d_pre, 0, 0).astype(BF)
        gn = dot(mean_ref[z], d_pre, 0, 0).astype(BF)
        g1_ref[2 * z, 0:COLS, :] = gs[0:COLS]
        g1_ref[2 * z + 1, 0:COLS, :] = gs[COLS:PAIR]
        g1_ref[2 * z, COLS:PAIR, :] = gn[0:COLS]
        g1_ref[2 * z + 1, COLS:PAIR, :] = gn[COLS:PAIR]
    high, low = split(x_ref[...])
    g2_ref[0:HID, :] = dot(hidden, d_ref[...], 0, 0)
    g2_ref[HID : 2 * HID, :] = dot(hidden, high, 0, 0) + dot(hidden, low, 0, 0)
    row = lax.broadcasted_iota(I32, (OWN, SEEDS), 0)
    for q in range(0, ND, 2):
        lanes = jnp.concatenate([send_ref[q : q + 1, :], send_ref[q + 1 : q + 2, :]], axis=1)
        hot = jnp.where(row == lanes, 1.0, 0.0).astype(BF)
        out_ref[q * SLOTS : (q + 2) * SLOTS, :] = dot(hot, hidden, 0, 0).astype(BF)
    hot = jnp.where(row == seed_ref[...], 1.0, 0.0).astype(BF)
    part_ref[...] = dot(dot(hot, hidden, 0, 0).astype(BF), w2s_ref[...])


def layer_body(in_ref, picks_ref, part_ref, w2n_ref, layer_ref):
    mean_two = (dot(picks_ref[...], in_ref[...], 0, 0) * (1.0 / K2)).astype(BF)
    layer_ref[...] = (part_ref[...] + dot(mean_two, w2n_ref[...])).astype(BF)


def swap(x, axis, groups=None):
    return lax.all_to_all(
        x, axis, split_axis=0, concat_axis=0, tiled=True, axis_index_groups=groups
    )


def to_all(x, axis, n):
    return swap(jnp.broadcast_to(x[None], (n,) + x.shape), axis)


def per_device(
    features, w1_self, w1_neigh, w2_self, w2_neigh, neigh_one, send_rows, recv_count,
    neigh_two, seed_rows, d_out,
):
    f = lax.axis_index("feat")
    q = lax.axis_index("dom")
    core = f % 2
    core_in = core.reshape(1)
    chips = [[2 * z + c for z in range(NZ)] for c in range(2)]
    own = features[0]
    other = lax.ppermute(own, "feat", [(i, i ^ 1) for i in range(NF)])

    w1 = jnp.concatenate([w1_self, w1_neigh], axis=0)
    piece = lax.dynamic_slice(w1, ((q // 2) * 16, (q % 2) * 128), (16, 128))
    piece = to_all(piece, "feat", NF)
    w1_all = to_all(piece, "dom", ND)

    send = send_rows[0, 0]
    seeds = seed_rows[0]
    grad_out = d_out[0, 0]
    picks, t_out = call(
        pick_body,
        "picks",
        (shape((ND, SLOTS, SEEDS), BF), shape((ND, SLOTS, HID), BF)),
        [SMEM, VMEM, VMEM],
    )(recv_count[:, 0, 0], neigh_two[0, 0].T, grad_out)
    t_in = swap(t_out, "dom")

    self_out = call(
        self_body,
        "self_rows",
        shape((NZ, OWN, PAIR), BF),
        [SMEM, VMEM, VMEM],
        [pltpu.VMEM((R1, PAIR), F32)],
    )(core_in, own, other)
    self_in = swap(self_out, "feat", chips)

    lists = neigh_one[0].reshape(K1, NZ, 2, OWN)
    lists = lax.dynamic_index_in_dim(lists, core, 2, keepdims=False).reshape(-1)
    mean_out = call(
        mean_body,
        "mean_rows",
        shape((NZ, OWN, PAIR), BF),
        [SMEM, VMEM, VMEM, SMEM],
        [pltpu.VMEM((NIN, PAIR), F32), pltpu.VMEM((HALF, PAIR), F32)],
    )(core_in, own, other, lists)
    mean_in = swap(mean_out, "feat", chips)

    x, d, d_hidden = call(
        owner_body,
        "owner_grads",
        (shape((OWN, HID), F32), shape((OWN, HID), BF), shape((OWN, HID), F32)),
        [VMEM] * 6,
    )(t_in.reshape(ND * SLOTS, HID), send, seeds, grad_out, w2_self, w2_neigh)

    g1, g2, outgoing, part = call(
        main_body,
        "project",
        (
            shape((NF, PAIR, HID), BF),
            shape((2 * HID, HID), F32),
            shape((ND * SLOTS, HID), BF),
            shape((SEEDS, HID), F32),
        ),
        [VMEM] * 9,
        [pltpu.VMEM((2, NF * COLS, HID), BF)],
    )(self_in, mean_in, w1_all, x, d, d_hidden, send, seeds, w2_self)

    g1 = jnp.sum(swap(g1, "feat").astype(F32), axis=0)
    g2 = jnp.sum(swap(g2.reshape(ND, 2 * HID // ND, HID), "dom"), axis=0)
    incoming = swap(outgoing.reshape(ND, SLOTS, HID), "dom").reshape(ND * SLOTS, HID)
    layer_out = call(layer_body, "layer_two", shape((SEEDS, HID), BF), [VMEM] * 4)(
        incoming, picks.reshape(ND * SLOTS, SEEDS), part, w2_neigh
    )

    g1 = jnp.sum(swap(g1.reshape(ND, PAIR // ND, HID), "dom"), axis=0)
    g2 = jnp.sum(to_all(g2, "feat", NF), axis=0)
    both = to_all(jnp.concatenate([g1, g2], axis=0), "dom", ND)
    g1 = both[:, : PAIR // ND].reshape(PAIR, HID)
    g2 = both[:, PAIR // ND :].reshape(2 * HID, HID)
    return (layer_out[None, None], g1[:COLS], g1[COLS:], g2[:HID], g2[HID:])


def solution(mesh):
    return jax.shard_map(
        per_device,
        mesh=mesh,
        in_specs=(
            P("dom", "feat", None),
            P("feat", None),
            P("feat", None),
            P(),
            P(),
            P("dom", None, None),
            P("dom", "feat", None, None),
            P(None, "feat", "dom"),
            P("dom", "feat", None, None),
            P("dom", "feat", None),
            P("dom", "feat", None, None),
        ),
        out_specs=(P("dom", "feat", None, None), P("feat", None), P("feat", None), P(), P()),
        check_vma=False,
    )
```

```python
import jax
import jax.numpy as jnp
from jax import lax
from jax.experimental import pallas as pl
from jax.experimental.pallas import tpu as pltpu
from jax.sharding import PartitionSpec as P

BF = jnp.bfloat16
F32 = jnp.float32
I32 = jnp.int32
NF = 16
ND = 16
NZ = 8
COLS = 64
PAIR = 128
NIN = 9216
R1 = 4608
OWN = 288
HALF = R1 // 2
K1 = 10
K2 = 15
SEEDS = 256
SLOTS = 128
HID = 256
UNROLL = 16
G2 = 256
G1 = 320
VMEM = pl.BlockSpec(memory_space=pltpu.VMEM)
SMEM = pl.BlockSpec(memory_space=pltpu.SMEM)


def call(body, name, outs, ins, scratch=(), limit=16, us=1):
    return pl.pallas_call(
        body,
        name=name,
        out_shape=outs,
        in_specs=ins,
        out_specs=jax.tree.map(lambda _: VMEM, outs),
        scratch_shapes=list(scratch),
        compiler_params=pltpu.CompilerParams(vmem_limit_bytes=limit << 20),
        cost_estimate=pl.CostEstimate(flops=us * 10**9, transcendentals=0, bytes_accessed=us * 10**6),
    )


def shape(dims, dtype):
    return jax.ShapeDtypeStruct(dims, dtype)


def dot(a, b, ca=1, cb=0):
    return lax.dot_general(a, b, (((ca,), (cb,)), ((), ())), preferred_element_type=F32)


def pick_body(count_ref, neigh_ref, dout_ref, picks_ref, t_ref):
    start = jnp.int32(0)
    lanes = neigh_ref[...]
    d_out = dout_ref[...]
    row = lax.broadcasted_iota(I32, (SLOTS, SEEDS), 0)
    for s in range(ND):
        count = count_ref[s]
        position = jnp.where(row < count, row + start, -1)
        total = jnp.zeros((SLOTS, SEEDS), F32)
        for k in range(K2):
            total = total + jnp.where(position == lanes[k : k + 1, :], 1.0, 0.0)
        picks = total.astype(BF)
        picks_ref[s] = picks
        t_ref[s] = dot(picks, d_out).astype(BF)
        start = start + count


def rows_body(core_ref, own_ref, other_ref, index_ref, out_ref, table, sums):
    core = core_ref[0]
    step = 512
    for c in range(0, NIN, step):
        both = jnp.concatenate([own_ref[:, c : c + step], other_ref[:, c : c + step]], axis=0)
        table[c : c + step, :] = both.astype(F32).T
    for z in range(NZ):
        first = pl.multiple_of((2 * z + core) * OWN, 32)
        out_ref[z, :, 0:PAIR] = table[pl.ds(first, OWN), :].astype(BF)

    def block(b, carry):
        z = b // (OWN // UNROLL)
        base = b * UNROLL + (z + core) * OWN
        for j in range(UNROLL):
            rows = [table[pl.ds(index_ref[k * R1 + base + j], 1), :] for k in range(K1)]
            while len(rows) > 1:
                even = len(rows) // 2 * 2
                rows = [rows[i] + rows[i + 1] for i in range(0, even, 2)] + rows[even:]
            sums[pl.ds(b * UNROLL + j, 1), :] = rows[0]
        return carry

    lax.fori_loop(0, HALF // UNROLL, block, 0)
    for z in range(NZ):
        mean = sums[z * OWN : (z + 1) * OWN, :] * (1.0 / K1)
        out_ref[z, :, PAIR : 2 * PAIR] = mean.astype(BF)


def split(x):
    high = x.astype(BF)
    return high, (x - high.astype(F32)).astype(BF)


def owner_body(t_ref, send_ref, seed_ref, dout_ref, w2s_ref, w2n_ref, x_ref, d_ref, dh_ref):
    d_out = dout_ref[...]
    row = lax.broadcasted_iota(I32, (OWN, SEEDS), 0)
    x = jnp.zeros((OWN, HID), F32)
    for q in range(0, ND, 2):
        lanes = jnp.concatenate([send_ref[q : q + 1, :], send_ref[q + 1 : q + 2, :]], axis=1)
        hot = jnp.where(row == lanes, 1.0, 0.0).astype(BF)
        x = x + dot(hot, t_ref[q * SLOTS : (q + 2) * SLOTS, :])
    x = x * (1.0 / K2)
    hot = jnp.where(row == seed_ref[...], 1.0, 0.0).astype(BF)
    d = dot(hot, d_out).astype(BF)
    high, low = split(x)
    w2n = w2n_ref[...]
    x_ref[...] = x
    d_ref[...] = d
    dh_ref[...] = dot(high, w2n, 1, 1) + dot(low, w2n, 1, 1) + dot(d, w2s_ref[...], 1, 1)


def reverse(j):
    return (j % 2) * 4 + (j // 2 % 2) * 2 + j // 4


def main_body(
    core_ref, rows_ref, wa_ref, wb_ref, x_ref, d_ref, dh_ref, send_ref, seed_ref, w2s_ref,
    out_ref, part_ref,
):
    core = core_ref[0]
    here = core_ref[1]
    chips = [jnp.bitwise_xor(here, reverse(j)) for j in range(NZ)]
    pre = jnp.zeros((OWN, HID), F32)
    for j in range(NZ):
        a, b = wa_ref[j], wb_ref[j]
        w = jnp.concatenate([a[:COLS], b[:COLS], a[COLS:], b[COLS:]], axis=0)
        pre = pre + dot(rows_ref[chips[j]], w)
    slope = jnp.exp(jnp.minimum(pre, 0.0))
    hidden = jnp.where(pre > 0, pre, slope - 1.0).astype(BF)
    d_pre = (dh_ref[...] * slope).astype(BF)
    for j in range(NZ):
        g = dot(rows_ref[chips[j]], d_pre, 0, 0).astype(BF)
        for q in range(ND):
            r, h = q // 2, q % 2
            at = (r // 4) * PAIR + (r % 4) * 16
            lanes = slice(h * 128, (h + 1) * 128)
            for side in range(2):
                f = 2 * chips[j] + (core if side == 0 else 1 - core)
                piece = g[at + side * COLS : at + side * COLS + 16, lanes]
                out_ref[q, pl.ds(pl.multiple_of(G1 + f * 16, 16), 16), :] = piece
    high, low = split(x_ref[...])
    g2s = dot(hidden, d_ref[...], 0, 0).astype(BF)
    g2n = (dot(hidden, high, 0, 0) + dot(hidden, low, 0, 0)).astype(BF)
    for q in range(ND):
        g = g2s if q < 8 else g2n
        for h in range(2):
            piece = g[(q % 8) * 32 : (q % 8) * 32 + 32, h * 128 : (h + 1) * 128]
            out_ref[q, G2 + h * 32 : G2 + h * 32 + 32, :] = piece
    row = lax.broadcasted_iota(I32, (OWN, SEEDS), 0)
    for q in range(0, ND, 2):
        lanes = jnp.concatenate([send_ref[q : q + 1, :], send_ref[q + 1 : q + 2, :]], axis=1)
        hot = jnp.where(row == lanes, 1.0, 0.0).astype(BF)
        listed = dot(hot, hidden, 0, 0).astype(BF)
        for i in range(2):
            for h in range(2):
                piece = listed[i * SLOTS : (i + 1) * SLOTS, h * 128 : (h + 1) * 128]
                out_ref[q + i, h * SLOTS : (h + 1) * SLOTS, :] = piece
    hot = jnp.where(row == seed_ref[...], 1.0, 0.0).astype(BF)
    part_ref[...] = dot(dot(hot, hidden, 0, 0).astype(BF), w2s_ref[...])


def first_sum_body(in_ref, out_ref):
    total = in_ref[0, G2:, :].astype(F32)
    for p in range(1, ND):
        total = total + in_ref[p, G2:, :].astype(F32)
    total = total.astype(BF)
    for f in range(NF):
        out_ref[f, 0:16, :] = total[G1 - G2 + f * 16 : G1 - G2 + f * 16 + 16]
        out_ref[f, 16:80, :] = total[0:64]


def second_sum_body(in_ref, out_ref):
    total = in_ref[0].astype(F32)
    for f in range(1, NF):
        total = total + in_ref[f].astype(F32)
    for q in range(ND):
        out_ref[q] = total


def place_body(in_ref, g1s_ref, g1n_ref, g2s_ref, g2n_ref):
    for q in range(ND):
        r, h = q // 2, q % 2
        g1 = g1s_ref if r < 4 else g1n_ref
        g1[(r % 4) * 16 : (r % 4) * 16 + 16, h * 128 : (h + 1) * 128] = in_ref[q, 0:16, :]
        g2 = g2s_ref if q < 8 else g2n_ref
        for half in range(2):
            piece = in_ref[q, 16 + half * 32 : 48 + half * 32, :]
            g2[(q % 8) * 32 : (q % 8) * 32 + 32, half * 128 : (half + 1) * 128] = piece


def layer_body(in_ref, picks_ref, part_ref, w2n_ref, layer_ref):
    total = part_ref[...]
    picks = picks_ref[...]
    for h in range(2):
        rows = in_ref[:, h * SLOTS : (h + 1) * SLOTS, :].reshape(ND * SLOTS, 128)
        mean = (dot(picks, rows, 0, 0) * (1.0 / K2)).astype(BF)
        total = total + dot(mean, w2n_ref[h * 128 : (h + 1) * 128, :])
    layer_ref[...] = total.astype(BF)


def swap(x, axis, groups=None):
    return lax.all_to_all(
        x, axis, split_axis=0, concat_axis=0, tiled=True, axis_index_groups=groups
    )


def fetch(x, bit):
    return lax.ppermute(x, "feat", [(i, i ^ bit) for i in range(NF)])


def per_device(
    features, w1_self, w1_neigh, w2_self, w2_neigh, neigh_one, send_rows, recv_count,
    neigh_two, seed_rows, d_out,
):
    f = lax.axis_index("feat")
    place = jnp.stack([jnp.bitwise_and(f, 1), jnp.right_shift(f, 1)])
    chips = [[2 * z + c for z in range(NZ)] for c in range(2)]
    own = features[0]
    other = fetch(own, 1)

    w1 = jnp.concatenate([w1_self, w1_neigh], axis=0)[None]
    w1 = jnp.concatenate([w1, fetch(w1, 8)], axis=0)
    w1 = jnp.concatenate([w1, fetch(w1, 4)], axis=0)
    place_early, w1 = lax.optimization_barrier((place, w1))
    w1 = jnp.concatenate([w1, fetch(w1, 2)], axis=0)
    w1_other = fetch(w1, 1)

    send = send_rows[0, 0]
    seeds = seed_rows[0]
    grad_out = d_out[0, 0]
    picks, t_out = call(
        pick_body,
        "picks",
        (shape((ND, SLOTS, SEEDS), BF), shape((ND, SLOTS, HID), BF)),
        [SMEM, VMEM, VMEM],
        us=5,
    )(recv_count[:, 0, 0], neigh_two[0, 0].T, grad_out)
    t_in = swap(t_out, "dom")

    rows_out = call(
        rows_body,
        "node_rows",
        shape((NZ, OWN, 2 * PAIR), BF),
        [SMEM, VMEM, VMEM, SMEM],
        [pltpu.VMEM((NIN, PAIR), F32), pltpu.VMEM((HALF, PAIR), F32)],
        limit=24,
        us=22,
    )(place_early, own, other, neigh_one.reshape(-1))
    rows_in = swap(rows_out, "feat", chips)

    x, d, d_hidden = call(
        owner_body,
        "owner_grads",
        (shape((OWN, HID), F32), shape((OWN, HID), BF), shape((OWN, HID), F32)),
        [VMEM] * 6,
    )(t_in.reshape(ND * SLOTS, HID), send, seeds, grad_out, w2_self, w2_neigh)

    to_dom, part = call(
        main_body,
        "project",
        (shape((ND, G1 + 256, 128), BF), shape((SEEDS, HID), F32)),
        [SMEM] + [VMEM] * 9,
        us=6,
    )(place, rows_in, w1, w1_other, x, d, d_hidden, send, seeds, w2_self)
    from_dom = swap(to_dom, "dom")

    to_feat = call(first_sum_body, "sum_dom", shape((NF, 80, 128), BF), [VMEM])(from_dom)
    from_feat = swap(to_feat, "feat")
    layer_out = call(layer_body, "layer_two", shape((SEEDS, HID), BF), [VMEM] * 4)(
        from_dom, picks.reshape(ND * SLOTS, SEEDS), part, w2_neigh
    )
    done = call(second_sum_body, "sum_feat", shape((ND, 80, 128), F32), [VMEM])(from_feat)
    done = swap(done, "dom")
    first = shape((COLS, HID), F32)
    second = shape((HID, HID), F32)
    grads = call(place_body, "place", (first, first, second, second), [VMEM])(done)
    return (layer_out[None, None], *grads)


def solution(mesh):
    return jax.shard_map(
        per_device,
        mesh=mesh,
        in_specs=(
            P("dom", "feat", None),
            P("feat", None),
            P("feat", None),
            P(),
            P(),
            P("dom", None, None),
            P("dom", "feat", None, None),
            P(None, "feat", "dom"),
            P("dom", "feat", None, None),
            P("dom", "feat", None),
            P("dom", "feat", None, None),
        ),
        out_specs=(P("dom", "feat", None, None), P("feat", None), P("feat", None), P(), P()),
        check_vma=False,
    )
```

```python
import jax
import jax.numpy as jnp
from jax import lax
from jax.experimental import pallas as pl
from jax.experimental.pallas import tpu as pltpu
from jax.sharding import PartitionSpec as P

BF = jnp.bfloat16
F32 = jnp.float32
I32 = jnp.int32
NF = 16
ND = 16
NZ = 8
COLS = 64
PAIR = 128
NIN = 9216
R1 = 4608
OWN = 288
HALF = R1 // 2
K1 = 10
K2 = 15
SEEDS = 256
SLOTS = 128
HID = 256
UNROLL = 16
G2 = 256
G1 = 320
VMEM = pl.BlockSpec(memory_space=pltpu.VMEM)
SMEM = pl.BlockSpec(memory_space=pltpu.SMEM)


def call(body, name, outs, ins, scratch=(), limit=16, us=1):
    return pl.pallas_call(
        body,
        name=name,
        out_shape=outs,
        in_specs=ins,
        out_specs=jax.tree.map(lambda _: VMEM, outs),
        scratch_shapes=list(scratch),
        compiler_params=pltpu.CompilerParams(vmem_limit_bytes=limit << 20),
        cost_estimate=pl.CostEstimate(flops=us * 10**9, transcendentals=0, bytes_accessed=us * 10**6),
    )


def shape(dims, dtype):
    return jax.ShapeDtypeStruct(dims, dtype)


def dot(a, b, ca=1, cb=0):
    return lax.dot_general(a, b, (((ca,), (cb,)), ((), ())), preferred_element_type=F32)


def pick_body(count_ref, neigh_ref, dout_ref, picks_ref, t_ref):
    start = jnp.int32(0)
    lanes = neigh_ref[...]
    d_out = dout_ref[...]
    row = lax.broadcasted_iota(I32, (SLOTS, SEEDS), 0)
    for s in range(ND):
        count = count_ref[s]
        position = jnp.where(row < count, row + start, -1)
        total = jnp.zeros((SLOTS, SEEDS), F32)
        for k in range(K2):
            total = total + jnp.where(position == lanes[k : k + 1, :], 1.0, 0.0)
        picks = total.astype(BF)
        picks_ref[s] = picks
        t = dot(picks, d_out).astype(BF)
        t_ref[s, 0:SLOTS, :] = t[:, 0:128]
        t_ref[s, SLOTS : 2 * SLOTS, :] = t[:, 128:256]
        start = start + count


def rows_body(core_ref, own_ref, other_ref, index_ref, out_ref, table, sums):
    core = core_ref[0]
    step = 512
    for c in range(0, NIN, step):
        both = jnp.concatenate([own_ref[:, c : c + step], other_ref[:, c : c + step]], axis=0)
        table[c : c + step, :] = both.astype(F32).T
    for z in range(NZ):
        first = pl.multiple_of((2 * z + core) * OWN, 32)
        out_ref[z, :, 0:PAIR] = table[pl.ds(first, OWN), :].astype(BF)

    def block(b, carry):
        z = b // (OWN // UNROLL)
        base = b * UNROLL + (z + core) * OWN
        for j in range(UNROLL):
            rows = [table[pl.ds(index_ref[k * R1 + base + j], 1), :] for k in range(K1)]
            while len(rows) > 1:
                even = len(rows) // 2 * 2
                rows = [rows[i] + rows[i + 1] for i in range(0, even, 2)] + rows[even:]
            sums[pl.ds(b * UNROLL + j, 1), :] = rows[0]
        return carry

    lax.fori_loop(0, HALF // UNROLL, block, 0)
    for z in range(NZ):
        mean = sums[z * OWN : (z + 1) * OWN, :] * (1.0 / K1)
        out_ref[z, :, PAIR : 2 * PAIR] = mean.astype(BF)


def split(x):
    high = x.astype(BF)
    return high, (x - high.astype(F32)).astype(BF)


def owner_grads(core, in_ref, send_ref, seed_ref, dout_ref, w2s_ref, w2n_ref, w_ref):
    d_out = dout_ref[...]
    row = lax.broadcasted_iota(I32, (OWN, SEEDS), 0)
    x = jnp.zeros((OWN, HID), F32)
    for q in range(0, ND, 2):
        lanes = jnp.concatenate([send_ref[q : q + 1, :], send_ref[q + 1 : q + 2, :]], axis=1)
        hot = jnp.where(row == lanes, 1.0, 0.0).astype(BF)
        t = jnp.concatenate(
            [
                jnp.concatenate([in_ref[i, 0:SLOTS, :], in_ref[i, SLOTS : 2 * SLOTS, :]], axis=1)
                for i in (q, q + 1)
            ],
            axis=0,
        )
        x = x + dot(hot, t)
    x = x * (1.0 / K2)
    hot = jnp.where(row == seed_ref[...], 1.0, 0.0).astype(BF)
    d = dot(hot, d_out).astype(BF)
    high, low = split(x)
    w2n = w2n_ref[...]
    d_hidden = dot(high, w2n, 1, 1) + dot(low, w2n, 1, 1) + dot(d, w2s_ref[...], 1, 1)
    for z in range(NZ):
        for side in range(2):
            f = 2 * z + (core if side == 0 else 1 - core)
            start = pl.multiple_of(2 * SLOTS + f * 16, 16)
            for q in range(ND):
                r, h = q // 2, q % 2
                at = (r // 4) * PAIR + side * COLS + (r % 4) * 16
                w_ref[z, at : at + 16, h * 128 : (h + 1) * 128] = in_ref[q, pl.ds(start, 16), :]
    return high, low, d, d_hidden


def main_body(
    core_ref, rows_ref, in_ref, send_ref, seed_ref, dout_ref, w2s_ref, w2n_ref,
    out_ref, part_ref, w_ref,
):
    core = core_ref[0]
    high, low, d, d_hidden = owner_grads(
        core, in_ref, send_ref, seed_ref, dout_ref, w2s_ref, w2n_ref, w_ref
    )
    pre = jnp.zeros((OWN, HID), F32)
    for z in range(NZ):
        pre = pre + dot(rows_ref[z], w_ref[z])
    slope = jnp.exp(jnp.minimum(pre, 0.0))
    hidden = jnp.where(pre > 0, pre, slope - 1.0).astype(BF)
    d_pre = (d_hidden * slope).astype(BF)
    for z in range(NZ):
        g = dot(rows_ref[z], d_pre, 0, 0).astype(BF)
        for q in range(ND):
            r, h = q // 2, q % 2
            at = (r // 4) * PAIR + (r % 4) * 16
            lanes = slice(h * 128, (h + 1) * 128)
            for side in range(2):
                f = 2 * z + (core if side == 0 else 1 - core)
                piece = g[at + side * COLS : at + side * COLS + 16, lanes]
                out_ref[q, pl.ds(pl.multiple_of(G1 + f * 16, 16), 16), :] = piece
    g2s = dot(hidden, d, 0, 0).astype(BF)
    g2n = (dot(hidden, high, 0, 0) + dot(hidden, low, 0, 0)).astype(BF)
    for q in range(ND):
        g = g2s if q < 8 else g2n
        for h in range(2):
            piece = g[(q % 8) * 32 : (q % 8) * 32 + 32, h * 128 : (h + 1) * 128]
            out_ref[q, G2 + h * 32 : G2 + h * 32 + 32, :] = piece
    row = lax.broadcasted_iota(I32, (OWN, SEEDS), 0)
    for q in range(0, ND, 2):
        lanes = jnp.concatenate([send_ref[q : q + 1, :], send_ref[q + 1 : q + 2, :]], axis=1)
        hot = jnp.where(row == lanes, 1.0, 0.0).astype(BF)
        listed = dot(hot, hidden, 0, 0).astype(BF)
        for i in range(2):
            for h in range(2):
                piece = listed[i * SLOTS : (i + 1) * SLOTS, h * 128 : (h + 1) * 128]
                out_ref[q + i, h * SLOTS : (h + 1) * SLOTS, :] = piece
    hot = jnp.where(row == seed_ref[...], 1.0, 0.0).astype(BF)
    part_ref[...] = dot(dot(hot, hidden, 0, 0).astype(BF), w2s_ref[...])


def first_sum_body(in_ref, out_ref):
    total = in_ref[0, G2:, :].astype(F32)
    for p in range(1, ND):
        total = total + in_ref[p, G2:, :].astype(F32)
    total = total.astype(BF)
    for f in range(NF):
        out_ref[f, 0:16, :] = total[G1 - G2 + f * 16 : G1 - G2 + f * 16 + 16]
        out_ref[f, 16:80, :] = total[0:64]


def second_sum_body(in_ref, out_ref):
    total = in_ref[0].astype(F32)
    for f in range(1, NF):
        total = total + in_ref[f].astype(F32)
    for q in range(ND):
        out_ref[q] = total


def place_body(in_ref, g1s_ref, g1n_ref, g2s_ref, g2n_ref):
    for q in range(ND):
        r, h = q // 2, q % 2
        g1 = g1s_ref if r < 4 else g1n_ref
        g1[(r % 4) * 16 : (r % 4) * 16 + 16, h * 128 : (h + 1) * 128] = in_ref[q, 0:16, :]
        g2 = g2s_ref if q < 8 else g2n_ref
        for half in range(2):
            piece = in_ref[q, 16 + half * 32 : 48 + half * 32, :]
            g2[(q % 8) * 32 : (q % 8) * 32 + 32, half * 128 : (half + 1) * 128] = piece


def layer_body(in_ref, picks_ref, part_ref, w2n_ref, layer_ref):
    total = part_ref[...]
    picks = picks_ref[...]
    for h in range(2):
        rows = in_ref[:, h * SLOTS : (h + 1) * SLOTS, :].reshape(ND * SLOTS, 128)
        mean = (dot(picks, rows, 0, 0) * (1.0 / K2)).astype(BF)
        total = total + dot(mean, w2n_ref[h * 128 : (h + 1) * 128, :])
    layer_ref[...] = total.astype(BF)


def swap(x, axis, groups=None):
    return lax.all_to_all(
        x, axis, split_axis=0, concat_axis=0, tiled=True, axis_index_groups=groups
    )


def fetch(x, bit):
    return lax.ppermute(x, "feat", [(i, i ^ bit) for i in range(NF)])


def per_device(
    features, w1_self, w1_neigh, w2_self, w2_neigh, neigh_one, send_rows, recv_count,
    neigh_two, seed_rows, d_out,
):
    f = lax.axis_index("feat")
    q = lax.axis_index("dom")
    core = jnp.bitwise_and(f, 1).reshape(1)
    chips = [[2 * z + c for z in range(NZ)] for c in range(2)]
    own = features[0]
    other = fetch(own, 1)

    w1 = jnp.concatenate([w1_self, w1_neigh], axis=0)
    start = (jnp.right_shift(q, 1) * 16, jnp.bitwise_and(q, 1) * 128)
    piece = lax.dynamic_slice(w1, start, (16, 128))
    piece = swap(jnp.broadcast_to(piece, (NF, 16, 128)), "feat").reshape(1, NF * 16, 128)

    send = send_rows[0, 0]
    seeds = seed_rows[0]
    grad_out = d_out[0, 0]
    picks, t_out = call(
        pick_body,
        "picks",
        (shape((ND, SLOTS, SEEDS), BF), shape((ND, 2 * SLOTS, 128), BF)),
        [SMEM, VMEM, VMEM],
        us=5,
    )(recv_count[:, 0, 0], neigh_two[0, 0].T, grad_out)
    piece = jnp.broadcast_to(piece, (ND, NF * 16, 128))
    t_in = swap(jnp.concatenate([t_out, piece], axis=1), "dom")

    rows_out = call(
        rows_body,
        "node_rows",
        shape((NZ, OWN, 2 * PAIR), BF),
        [SMEM, VMEM, VMEM, SMEM],
        [pltpu.VMEM((NIN, PAIR), F32), pltpu.VMEM((HALF, PAIR), F32)],
        limit=24,
        us=22,
    )(core, own, other, neigh_one.reshape(-1))
    rows_in = swap(rows_out, "feat", chips)

    to_dom, part = call(
        main_body,
        "project",
        (shape((ND, G1 + 256, 128), BF), shape((SEEDS, HID), F32)),
        [SMEM] + [VMEM] * 7,
        [pltpu.VMEM((NZ, 2 * PAIR, HID), BF)],
        us=4,
    )(core, rows_in, t_in, send, seeds, grad_out, w2_self, w2_neigh)
    from_dom = swap(to_dom, "dom")

    to_feat = call(first_sum_body, "sum_dom", shape((NF, 80, 128), BF), [VMEM])(from_dom)
    from_feat = swap(to_feat, "feat")
    layer_out = call(layer_body, "layer_two", shape((SEEDS, HID), BF), [VMEM] * 4)(
        from_dom, picks.reshape(ND * SLOTS, SEEDS), part, w2_neigh
    )
    done = call(second_sum_body, "sum_feat", shape((ND, 80, 128), F32), [VMEM])(from_feat)
    done = swap(done, "dom")
    first = shape((COLS, HID), F32)
    second = shape((HID, HID), F32)
    grads = call(place_body, "place", (first, first, second, second), [VMEM])(done)
    return (layer_out[None, None], *grads)


def solution(mesh):
    return jax.shard_map(
        per_device,
        mesh=mesh,
        in_specs=(
            P("dom", "feat", None),
            P("feat", None),
            P("feat", None),
            P(),
            P(),
            P("dom", None, None),
            P("dom", "feat", None, None),
            P(None, "feat", "dom"),
            P("dom", "feat", None, None),
            P("dom", "feat", None),
            P("dom", "feat", None, None),
        ),
        out_specs=(P("dom", "feat", None, None), P("feat", None), P("feat", None), P(), P()),
        check_vma=False,
    )
```

```python
import jax
import jax.numpy as jnp
from jax import lax
from jax.experimental import pallas as pl
from jax.experimental.pallas import tpu as pltpu
from jax.sharding import PartitionSpec as P

BF = jnp.bfloat16
F32 = jnp.float32
I32 = jnp.int32
NF = 16
ND = 16
NZ = 8
COLS = 64
PAIR = 128
NIN = 9216
R1 = 4608
OWN = 288
HALF = R1 // 2
K1 = 10
K2 = 15
SEEDS = 256
SLOTS = 128
HID = 256
UNROLL = 16
G2 = 256
G1 = 320
VMEM = pl.BlockSpec(memory_space=pltpu.VMEM)
SMEM = pl.BlockSpec(memory_space=pltpu.SMEM)


def call(body, name, outs, ins, scratch=(), limit=16, us=1):
    return pl.pallas_call(
        body,
        name=name,
        out_shape=outs,
        in_specs=ins,
        out_specs=jax.tree.map(lambda _: VMEM, outs),
        scratch_shapes=list(scratch),
        compiler_params=pltpu.CompilerParams(vmem_limit_bytes=limit << 20),
        cost_estimate=pl.CostEstimate(flops=us * 10**9, transcendentals=0, bytes_accessed=us * 10**6),
    )


def shape(dims, dtype):
    return jax.ShapeDtypeStruct(dims, dtype)


def dot(a, b, ca=1, cb=0):
    return lax.dot_general(a, b, (((ca,), (cb,)), ((), ())), preferred_element_type=F32)


def picks_of(source, start, count_ref, lanes):
    count = count_ref[source]
    row = lax.broadcasted_iota(I32, (SLOTS, SEEDS), 0)
    position = jnp.where(row < count, row + start, -1)
    total = jnp.zeros((SLOTS, SEEDS), F32)
    for k in range(K2):
        total = total + jnp.where(position == lanes[k : k + 1, :], 1.0, 0.0)
    return total.astype(BF), start + count


def pick_body(count_ref, neigh_ref, dout_ref, t_ref):
    start = jnp.int32(0)
    lanes = neigh_ref[...]
    d_out = dout_ref[...]
    for s in range(ND):
        picks, start = picks_of(s, start, count_ref, lanes)
        t = dot(picks, d_out).astype(BF)
        t_ref[s, 0:SLOTS, :] = t[:, 0:128]
        t_ref[s, SLOTS : 2 * SLOTS, :] = t[:, 128:256]


def rows_body(core_ref, own_ref, other_ref, index_ref, out_ref, table, sums):
    core = core_ref[0]
    step = 512
    for c in range(0, NIN, step):
        both = jnp.concatenate([own_ref[:, c : c + step], other_ref[:, c : c + step]], axis=0)
        table[c : c + step, :] = both.astype(F32).T
    for z in range(NZ):
        first = pl.multiple_of((2 * z + core) * OWN, 32)
        out_ref[z, :, 0:PAIR] = table[pl.ds(first, OWN), :].astype(BF)

    def block(b, carry):
        z = b // (OWN // UNROLL)
        base = b * UNROLL + (z + core) * OWN
        for j in range(UNROLL):
            rows = [table[pl.ds(index_ref[k * R1 + base + j], 1), :] for k in range(K1)]
            while len(rows) > 1:
                even = len(rows) // 2 * 2
                rows = [rows[i] + rows[i + 1] for i in range(0, even, 2)] + rows[even:]
            sums[pl.ds(b * UNROLL + j, 1), :] = rows[0]
        return carry

    lax.fori_loop(0, HALF // UNROLL, block, 0)
    for z in range(NZ):
        mean = sums[z * OWN : (z + 1) * OWN, :] * (1.0 / K1)
        out_ref[z, :, PAIR : 2 * PAIR] = mean.astype(BF)


def split(x):
    high = x.astype(BF)
    return high, (x - high.astype(F32)).astype(BF)


def owner_grads(in_ref, other_ref, send_ref, seed_ref, dout_ref, w2s_ref, w2n_ref, w_ref):
    d_out = dout_ref[...]
    row = lax.broadcasted_iota(I32, (OWN, SEEDS), 0)
    x = jnp.zeros((OWN, HID), F32)
    for q in range(0, ND, 2):
        lanes = jnp.concatenate([send_ref[q : q + 1, :], send_ref[q + 1 : q + 2, :]], axis=1)
        hot = jnp.where(row == lanes, 1.0, 0.0).astype(BF)
        t = jnp.concatenate(
            [
                jnp.concatenate([in_ref[i, 0:SLOTS, :], in_ref[i, SLOTS : 2 * SLOTS, :]], axis=1)
                for i in (q, q + 1)
            ],
            axis=0,
        )
        x = x + dot(hot, t)
    x = x * (1.0 / K2)
    hot = jnp.where(row == seed_ref[...], 1.0, 0.0).astype(BF)
    d = dot(hot, d_out).astype(BF)
    high, low = split(x)
    w2n = w2n_ref[...]
    d_hidden = dot(high, w2n, 1, 1) + dot(low, w2n, 1, 1) + dot(d, w2s_ref[...], 1, 1)
    for z in range(NZ):
        for q in range(ND):
            r, h = q // 2, q % 2
            at = (r // 4) * PAIR + (r % 4) * 16
            lanes = slice(h * 128, (h + 1) * 128)
            own = in_ref[q, 2 * SLOTS + z * 16 : 2 * SLOTS + z * 16 + 16, :]
            w_ref[z, at : at + 16, lanes] = own
            w_ref[z, at + COLS : at + COLS + 16, lanes] = other_ref[q, z * 16 : z * 16 + 16, :]
    return high, low, d, d_hidden


def main_body(
    core_ref, rows_ref, in_ref, other_ref, send_ref, seed_ref, dout_ref, w2s_ref, w2n_ref,
    out_ref, part_ref, w_ref,
):
    core = core_ref[0]
    high, low, d, d_hidden = owner_grads(
        in_ref, other_ref, send_ref, seed_ref, dout_ref, w2s_ref, w2n_ref, w_ref
    )
    pre = jnp.zeros((OWN, HID), F32)
    for z in range(NZ):
        pre = pre + dot(rows_ref[z], w_ref[z])
    slope = jnp.exp(jnp.minimum(pre, 0.0))
    hidden = jnp.where(pre > 0, pre, slope - 1.0).astype(BF)
    d_pre = (d_hidden * slope).astype(BF)
    for z in range(NZ):
        g = dot(rows_ref[z], d_pre, 0, 0).astype(BF)
        for q in range(ND):
            r, h = q // 2, q % 2
            at = (r // 4) * PAIR + (r % 4) * 16
            lanes = slice(h * 128, (h + 1) * 128)
            for side in range(2):
                f = 2 * z + (core if side == 0 else 1 - core)
                piece = g[at + side * COLS : at + side * COLS + 16, lanes]
                out_ref[q, pl.ds(pl.multiple_of(G1 + f * 16, 16), 16), :] = piece
    g2s = dot(hidden, d, 0, 0).astype(BF)
    g2n = (dot(hidden, high, 0, 0) + dot(hidden, low, 0, 0)).astype(BF)
    for q in range(ND):
        g = g2s if q < 8 else g2n
        for h in range(2):
            piece = g[(q % 8) * 32 : (q % 8) * 32 + 32, h * 128 : (h + 1) * 128]
            out_ref[q, G2 + h * 32 : G2 + h * 32 + 32, :] = piece
    row = lax.broadcasted_iota(I32, (OWN, SEEDS), 0)
    for q in range(0, ND, 2):
        lanes = jnp.concatenate([send_ref[q : q + 1, :], send_ref[q + 1 : q + 2, :]], axis=1)
        hot = jnp.where(row == lanes, 1.0, 0.0).astype(BF)
        listed = dot(hot, hidden, 0, 0).astype(BF)
        for i in range(2):
            for h in range(2):
                piece = listed[i * SLOTS : (i + 1) * SLOTS, h * 128 : (h + 1) * 128]
                out_ref[q + i, h * SLOTS : (h + 1) * SLOTS, :] = piece
    hot = jnp.where(row == seed_ref[...], 1.0, 0.0).astype(BF)
    part_ref[...] = dot(dot(hot, hidden, 0, 0).astype(BF), w2s_ref[...])


def first_sum_body(in_ref, out_ref):
    total = in_ref[0, G2:, :].astype(F32)
    for p in range(1, ND):
        total = total + in_ref[p, G2:, :].astype(F32)
    total = total.astype(BF)
    for f in range(NF):
        out_ref[f, 0:16, :] = total[G1 - G2 + f * 16 : G1 - G2 + f * 16 + 16]
        out_ref[f, 16:80, :] = total[0:64]


def second_sum_body(in_ref, out_ref):
    total = in_ref[0].astype(F32)
    for f in range(1, NF):
        total = total + in_ref[f].astype(F32)
    total = total.astype(BF)
    for q in range(ND):
        out_ref[q] = total


def place_body(in_ref, g1s_ref, g1n_ref, g2s_ref, g2n_ref):
    for q in range(ND):
        r, h = q // 2, q % 2
        g1 = g1s_ref if r < 4 else g1n_ref
        g1[(r % 4) * 16 : (r % 4) * 16 + 16, h * 128 : (h + 1) * 128] = in_ref[q, 0:16, :].astype(F32)
        g2 = g2s_ref if q < 8 else g2n_ref
        for half in range(2):
            piece = in_ref[q, 16 + half * 32 : 48 + half * 32, :].astype(F32)
            g2[(q % 8) * 32 : (q % 8) * 32 + 32, half * 128 : (half + 1) * 128] = piece


def layer_body(count_ref, neigh_ref, in_ref, part_ref, w2n_ref, layer_ref):
    start = jnp.int32(0)
    names = neigh_ref[...]
    total = jnp.zeros((SEEDS, HID), F32)
    for s in range(ND):
        picks, start = picks_of(s, start, count_ref, names)
        rows = [in_ref[s, 0:SLOTS, :], in_ref[s, SLOTS : 2 * SLOTS, :]]
        total = total + dot(picks, jnp.concatenate(rows, axis=1), 0, 0)
    mean_two = (total * (1.0 / K2)).astype(BF)
    layer_ref[...] = (part_ref[...] + dot(mean_two, w2n_ref[...])).astype(BF)


def swap(x, axis, groups=None):
    return lax.all_to_all(
        x, axis, split_axis=0, concat_axis=0, tiled=True, axis_index_groups=groups
    )


def fetch(x, bit):
    return lax.ppermute(x, "feat", [(i, i ^ bit) for i in range(NF)])


def per_device(
    features, w1_self, w1_neigh, w2_self, w2_neigh, neigh_one, send_rows, recv_count,
    neigh_two, seed_rows, d_out,
):
    f = lax.axis_index("feat")
    q = lax.axis_index("dom")
    core = jnp.bitwise_and(f, 1).reshape(1)
    chips = [[2 * z + c for z in range(NZ)] for c in range(2)]
    own = features[0]
    other = fetch(own, 1)

    w1 = jnp.concatenate([w1_self, w1_neigh], axis=0)
    start = (jnp.right_shift(q, 1) * 16, jnp.bitwise_and(q, 1) * 128)
    piece = lax.dynamic_slice(w1, start, (16, 128))
    piece = swap(jnp.broadcast_to(piece, (NZ, 16, 128)), "feat", chips).reshape(1, NZ * 16, 128)

    send = send_rows[0, 0]
    seeds = seed_rows[0]
    grad_out = d_out[0, 0]
    counts = recv_count[:, 0, 0]
    names = neigh_two[0, 0].T
    t_out = call(
        pick_body, "picks", shape((ND, 2 * SLOTS, 128), BF), [SMEM, VMEM, VMEM], limit=60, us=5
    )(counts, names, grad_out)
    piece = jnp.broadcast_to(piece, (ND, NZ * 16, 128))
    t_in = swap(jnp.concatenate([t_out, piece], axis=1), "dom")
    w1_other = fetch(t_in[:, 2 * SLOTS :], 1)

    rows_out = call(
        rows_body,
        "node_rows",
        shape((NZ, OWN, 2 * PAIR), BF),
        [SMEM, VMEM, VMEM, SMEM],
        [pltpu.VMEM((NIN, PAIR), F32), pltpu.VMEM((HALF, PAIR), F32)],
        limit=60,
        us=22,
    )(core, own, other, neigh_one.reshape(-1))
    rows_in = swap(rows_out, "feat", chips)

    to_dom, part = call(
        main_body,
        "project",
        (shape((ND, G1 + 256, 128), BF), shape((SEEDS, HID), F32)),
        [SMEM] + [VMEM] * 8,
        [pltpu.VMEM((NZ, 2 * PAIR, HID), BF)],
        us=4,
    )(core, rows_in, t_in, w1_other, send, seeds, grad_out, w2_self, w2_neigh)
    from_dom = swap(to_dom, "dom")

    to_feat = call(first_sum_body, "sum_dom", shape((NF, 80, 128), BF), [VMEM])(from_dom)
    from_feat = swap(to_feat, "feat")
    layer_out = call(
        layer_body,
        "layer_two",
        shape((SEEDS, HID), BF),
        [SMEM] + [VMEM] * 4,
        limit=60,
        us=5,
    )(counts, names, from_dom, part, w2_neigh)
    done = call(second_sum_body, "sum_feat", shape((ND, 80, 128), BF), [VMEM], limit=60)(from_feat)
    done = swap(done, "dom")
    first = shape((COLS, HID), F32)
    second = shape((HID, HID), F32)
    grads = call(place_body, "place", (first, first, second, second), [VMEM])(done)
    return (layer_out[None, None], *grads)


def solution(mesh):
    return jax.shard_map(
        per_device,
        mesh=mesh,
        in_specs=(
            P("dom", "feat", None),
            P("feat", None),
            P("feat", None),
            P(),
            P(),
            P("dom", None, None),
            P("dom", "feat", None, None),
            P(None, "feat", "dom"),
            P("dom", "feat", None, None),
            P("dom", "feat", None),
            P("dom", "feat", None, None),
        ),
        out_specs=(P("dom", "feat", None, None), P("feat", None), P("feat", None), P(), P()),
        check_vma=False,
    )
```

```python
import jax
import jax.numpy as jnp
from jax import lax
from jax.experimental import pallas as pl
from jax.experimental.pallas import tpu as pltpu
from jax.sharding import PartitionSpec as P

BF = jnp.bfloat16
F32 = jnp.float32
I32 = jnp.int32
NF = 16
ND = 16
NZ = 8
COLS = 64
PAIR = 128
NIN = 9216
R1 = 4608
OWN = 288
HALF = R1 // 2
K1 = 10
K2 = 15
SEEDS = 256
SLOTS = 128
HID = 256
UNROLL = 16
G2 = 256
RING = (0, -1, 1, -2, 2, -3, 3, -4)
VMEM = pl.BlockSpec(memory_space=pltpu.VMEM)
SMEM = pl.BlockSpec(memory_space=pltpu.SMEM)


def call(body, name, outs, ins, scratch=(), limit=16, us=1):
    return pl.pallas_call(
        body,
        name=name,
        out_shape=outs,
        in_specs=ins,
        out_specs=jax.tree.map(lambda _: VMEM, outs),
        scratch_shapes=list(scratch),
        compiler_params=pltpu.CompilerParams(vmem_limit_bytes=limit << 20),
        cost_estimate=pl.CostEstimate(flops=us * 10**9, transcendentals=0, bytes_accessed=us * 10**6),
    )


def shape(dims, dtype):
    return jax.ShapeDtypeStruct(dims, dtype)


def dot(a, b, ca=1, cb=0):
    return lax.dot_general(a, b, (((ca,), (cb,)), ((), ())), preferred_element_type=F32)


def picks_of(source, start, count_ref, lanes):
    count = count_ref[source]
    row = lax.broadcasted_iota(I32, (SLOTS, SEEDS), 0)
    position = jnp.where(row < count, row + start, -1)
    total = jnp.zeros((SLOTS, SEEDS), F32)
    for k in range(K2):
        total = total + jnp.where(position == lanes[k : k + 1, :], 1.0, 0.0)
    return total.astype(BF), start + count


def pick_body(count_ref, neigh_ref, dout_ref, t_ref):
    start = jnp.int32(0)
    lanes = neigh_ref[...]
    d_out = dout_ref[...]
    for s in range(ND):
        picks, start = picks_of(s, start, count_ref, lanes)
        t_ref[s] = dot(picks, d_out).astype(BF)


def rows_body(
    core_ref, own_ref, other_ref, index_ref, w_ref, wo_ref, out_ref, part_ref, table, sums
):
    core = core_ref[0]
    step = 512
    for c in range(0, NIN, step):
        both = jnp.concatenate([own_ref[:, c : c + step], other_ref[:, c : c + step]], axis=0)
        table[c : c + step, :] = both.astype(F32).T
    for z in range(NZ):
        first = pl.multiple_of((2 * z + core) * OWN, 32)
        out_ref[z, :, 0:PAIR] = table[pl.ds(first, OWN), :].astype(BF)

    def block(b, carry):
        z = b // (OWN // UNROLL)
        base = b * UNROLL + (z + core) * OWN
        for j in range(UNROLL):
            rows = [table[pl.ds(index_ref[k * R1 + base + j], 1), :] for k in range(K1)]
            while len(rows) > 1:
                even = len(rows) // 2 * 2
                rows = [rows[i] + rows[i + 1] for i in range(0, even, 2)] + rows[even:]
            sums[pl.ds(b * UNROLL + j, 1), :] = rows[0]
        return carry

    lax.fori_loop(0, HALF // UNROLL, block, 0)
    a, b = w_ref[...], wo_ref[...]
    w = jnp.concatenate([a[:COLS], b[:COLS], a[COLS:], b[COLS:]], axis=0)
    for z in range(NZ):
        mean = sums[z * OWN : (z + 1) * OWN, :] * (1.0 / K1)
        out_ref[z, :, PAIR : 2 * PAIR] = mean.astype(BF)
        part_ref[z] = dot(out_ref[z], w).astype(BF)


def split(x):
    high = x.astype(BF)
    return high, (x - high.astype(F32)).astype(BF)


def owner_grads(in_ref, send_ref, seed_ref, dout_ref, w2s_ref, w2n_ref):
    row = lax.broadcasted_iota(I32, (OWN, SEEDS), 0)
    x = jnp.zeros((OWN, HID), F32)
    for q in range(0, ND, 2):
        lanes = jnp.concatenate([send_ref[q : q + 1, :], send_ref[q + 1 : q + 2, :]], axis=1)
        hot = jnp.where(row == lanes, 1.0, 0.0).astype(BF)
        x = x + dot(hot, in_ref[q : q + 2].reshape(2 * SLOTS, HID))
    x = x * (1.0 / K2)
    hot = jnp.where(row == seed_ref[...], 1.0, 0.0).astype(BF)
    d = dot(hot, dout_ref[...]).astype(BF)
    high, low = split(x)
    w2n = w2n_ref[...]
    d_hidden = dot(high, w2n, 1, 1) + dot(low, w2n, 1, 1) + dot(d, w2s_ref[...], 1, 1)
    return high, low, d, d_hidden


def main_body(
    share_ref, in_ref, send_ref, seed_ref, dout_ref, w2s_ref, w2n_ref,
    out_ref, part_ref, dpre_ref,
):
    high, low, d, d_hidden = owner_grads(in_ref, send_ref, seed_ref, dout_ref, w2s_ref, w2n_ref)
    pre = share_ref[0].astype(F32)
    for z in range(1, NZ):
        pre = pre + share_ref[z].astype(F32)
    slope = jnp.exp(jnp.minimum(pre, 0.0))
    hidden = jnp.where(pre > 0, pre, slope - 1.0).astype(BF)
    dpre_ref[...] = (d_hidden * slope).astype(BF)
    g2s = dot(hidden, d, 0, 0).astype(BF)
    g2n = (dot(hidden, high, 0, 0) + dot(hidden, low, 0, 0)).astype(BF)
    for q in range(ND):
        g = g2s if q < 8 else g2n
        for h in range(2):
            piece = g[(q % 8) * 32 : (q % 8) * 32 + 32, h * 128 : (h + 1) * 128]
            out_ref[q, G2 + h * 32 : G2 + h * 32 + 32, :] = piece
    row = lax.broadcasted_iota(I32, (OWN, SEEDS), 0)
    for q in range(0, ND, 2):
        lanes = jnp.concatenate([send_ref[q : q + 1, :], send_ref[q + 1 : q + 2, :]], axis=1)
        hot = jnp.where(row == lanes, 1.0, 0.0).astype(BF)
        listed = dot(hot, hidden, 0, 0).astype(BF)
        for i in range(2):
            for h in range(2):
                piece = listed[i * SLOTS : (i + 1) * SLOTS, h * 128 : (h + 1) * 128]
                out_ref[q + i, h * SLOTS : (h + 1) * SLOTS, :] = piece
    hot = jnp.where(row == seed_ref[...], 1.0, 0.0).astype(BF)
    part_ref[...] = dot(dot(hot, hidden, 0, 0).astype(BF), w2s_ref[...])


def columns_body(chip_ref, rows_ref, *refs):
    keep_ref, give_ref = refs[NZ:]
    chip = chip_ref[0]
    total = jnp.zeros((2 * PAIR, HID), F32)
    for i, offset in enumerate(RING):
        source = jnp.bitwise_and(chip + offset, NZ - 1)
        total = total + dot(rows_ref[source], refs[i][...], 0, 0)
    keep_ref[0:COLS, :] = total[0:COLS]
    keep_ref[COLS:PAIR, :] = total[PAIR : PAIR + COLS]
    give_ref[0:COLS, :] = total[COLS:PAIR]
    give_ref[COLS:PAIR, :] = total[PAIR + COLS :]


def pair_sum_body(keep_ref, got_ref, out_ref):
    total = keep_ref[...] + got_ref[...]
    for q in range(ND):
        r, h = q // 2, q % 2
        out_ref[q] = total[r * 16 : r * 16 + 16, h * 128 : (h + 1) * 128]


def first_sum_body(in_ref, out_ref):
    total = in_ref[0, G2:, :].astype(F32)
    for p in range(1, ND):
        total = total + in_ref[p, G2:, :].astype(F32)
    total = total.astype(BF)
    for f in range(NF):
        out_ref[f] = total


def second_sum_body(one_ref, two_ref, out_ref):
    one = one_ref[0]
    two = two_ref[0].astype(F32)
    for f in range(1, NF):
        one = one + one_ref[f]
        two = two + two_ref[f].astype(F32)
    both = jnp.concatenate([one, two], axis=0).astype(BF)
    for q in range(ND):
        out_ref[q] = both


def place_body(in_ref, g1s_ref, g1n_ref, g2s_ref, g2n_ref):
    for q in range(ND):
        r, h = q // 2, q % 2
        g1 = g1s_ref if r < 4 else g1n_ref
        g1[(r % 4) * 16 : (r % 4) * 16 + 16, h * 128 : (h + 1) * 128] = in_ref[q, 0:16, :].astype(F32)
        g2 = g2s_ref if q < 8 else g2n_ref
        for half in range(2):
            piece = in_ref[q, 16 + half * 32 : 48 + half * 32, :].astype(F32)
            g2[(q % 8) * 32 : (q % 8) * 32 + 32, half * 128 : (half + 1) * 128] = piece


def layer_body(count_ref, neigh_ref, in_ref, part_ref, w2n_ref, layer_ref):
    start = jnp.int32(0)
    names = neigh_ref[...]
    total = jnp.zeros((SEEDS, HID), F32)
    for s in range(ND):
        picks, start = picks_of(s, start, count_ref, names)
        rows = [in_ref[s, 0:SLOTS, :], in_ref[s, SLOTS : 2 * SLOTS, :]]
        total = total + dot(picks, jnp.concatenate(rows, axis=1), 0, 0)
    mean_two = (total * (1.0 / K2)).astype(BF)
    layer_ref[...] = (part_ref[...] + dot(mean_two, w2n_ref[...])).astype(BF)


def swap(x, axis, groups=None):
    return lax.all_to_all(
        x, axis, split_axis=0, concat_axis=0, tiled=True, axis_index_groups=groups
    )


def turn(x, step):
    return lax.ppermute(x, "feat", [(i, (i + 2 * step) % NF) for i in range(NF)])


def fetch(x, bit):
    return lax.ppermute(x, "feat", [(i, i ^ bit) for i in range(NF)])


def per_device(
    features, w1_self, w1_neigh, w2_self, w2_neigh, neigh_one, send_rows, recv_count,
    neigh_two, seed_rows, d_out,
):
    f = lax.axis_index("feat")
    core = jnp.bitwise_and(f, 1).reshape(1)
    chip = jnp.right_shift(f, 1).reshape(1)
    chips = [[2 * z + c for z in range(NZ)] for c in range(2)]
    own = features[0]
    other = fetch(own, 1)
    w1 = jnp.concatenate([w1_self, w1_neigh], axis=0)
    w1_other = fetch(w1, 1)

    send = send_rows[0, 0]
    seeds = seed_rows[0]
    grad_out = d_out[0, 0]
    counts = recv_count[:, 0, 0]
    names = neigh_two[0, 0].T
    t_out = call(
        pick_body, "picks", shape((ND, SLOTS, HID), BF), [SMEM, VMEM, VMEM], limit=60, us=5
    )(counts, names, grad_out)
    t_in = swap(t_out, "dom")

    rows = shape((NZ, OWN, 2 * PAIR), BF)
    rows, share = call(
        rows_body,
        "node_rows",
        (rows, rows),
        [SMEM, VMEM, VMEM, SMEM, VMEM, VMEM],
        [pltpu.VMEM((NIN, PAIR), F32), pltpu.VMEM((HALF, PAIR), F32)],
        limit=60,
        us=22,
    )(core, own, other, neigh_one.reshape(-1), w1, w1_other)
    share = swap(share, "feat", chips)

    to_dom, part, d_pre = call(
        main_body,
        "project",
        (
            shape((ND, G2 + 64, 128), BF),
            shape((SEEDS, HID), F32),
            shape((OWN, HID), BF),
        ),
        [VMEM] * 7,
        us=4,
    )(share, t_in, send, seeds, grad_out, w2_self, w2_neigh)

    ring = {0: d_pre}
    for i in range(1, 4):
        ring[-i] = turn(ring[1 - i], 1)
        ring[i] = turn(ring[i - 1], -1)
    ring[-4] = turn(ring[-3], 1)
    from_dom = swap(to_dom, "dom")

    keep, give = call(
        columns_body,
        "columns",
        (shape((PAIR, HID), F32), shape((PAIR, HID), F32)),
        [SMEM] + [VMEM] * (1 + NZ),
        us=2,
    )(chip, rows, *[ring[i] for i in RING])
    one = call(pair_sum_body, "sum_pair", shape((ND, 16, 128), F32), [VMEM] * 2)(
        keep, fetch(give, 1)
    )

    two = call(first_sum_body, "sum_dom", shape((NF, 64, 128), BF), [VMEM])(from_dom)
    two = swap(two, "feat")
    one = swap(one, "dom")
    layer_out = call(
        layer_body,
        "layer_two",
        shape((SEEDS, HID), BF),
        [SMEM] + [VMEM] * 4,
        limit=60,
        us=5,
    )(counts, names, from_dom, part, w2_neigh)
    done = call(
        second_sum_body, "sum_all", shape((ND, 80, 128), BF), [VMEM] * 2, limit=60
    )(one, two)
    done = swap(done, "dom")
    first = shape((COLS, HID), F32)
    second = shape((HID, HID), F32)
    grads = call(place_body, "place", (first, first, second, second), [VMEM])(done)
    return (layer_out[None, None], *grads)


def solution(mesh):
    return jax.shard_map(
        per_device,
        mesh=mesh,
        in_specs=(
            P("dom", "feat", None),
            P("feat", None),
            P("feat", None),
            P(),
            P(),
            P("dom", None, None),
            P("dom", "feat", None, None),
            P(None, "feat", "dom"),
            P("dom", "feat", None, None),
            P("dom", "feat", None),
            P("dom", "feat", None, None),
        ),
        out_specs=(P("dom", "feat", None, None), P("feat", None), P("feat", None), P(), P()),
        check_vma=False,
    )
```

```python
import jax
import jax.numpy as jnp
from jax import lax
from jax.experimental import pallas as pl
from jax.experimental.pallas import tpu as pltpu
from jax.sharding import PartitionSpec as P

BF = jnp.bfloat16
F32 = jnp.float32
I32 = jnp.int32
NF = 16
ND = 16
NZ = 8
COLS = 64
PAIR = 128
NIN = 9216
R1 = 4608
OWN = 288
HALF = R1 // 2
K1 = 10
K2 = 15
SEEDS = 256
SLOTS = 128
HID = 256
UNROLL = 16
G2 = 256
RING = (0, -1, 1, -2, 2, -3, 3, -4)
VMEM = pl.BlockSpec(memory_space=pltpu.VMEM)
SMEM = pl.BlockSpec(memory_space=pltpu.SMEM)


def call(body, name, outs, ins, scratch=(), limit=16, us=1):
    return pl.pallas_call(
        body,
        name=name,
        out_shape=outs,
        in_specs=ins,
        out_specs=jax.tree.map(lambda _: VMEM, outs),
        scratch_shapes=list(scratch),
        compiler_params=pltpu.CompilerParams(vmem_limit_bytes=limit << 20),
        cost_estimate=pl.CostEstimate(flops=us * 10**9, transcendentals=0, bytes_accessed=us * 10**6),
    )


def shape(dims, dtype):
    return jax.ShapeDtypeStruct(dims, dtype)


def dot(a, b, ca=1, cb=0):
    return lax.dot_general(a, b, (((ca,), (cb,)), ((), ())), preferred_element_type=F32)


def picks_of(source, start, count_ref, lanes):
    count = count_ref[source]
    row = lax.broadcasted_iota(I32, (SLOTS, SEEDS), 0)
    position = jnp.where(row < count, row + start, -1)
    total = jnp.zeros((SLOTS, SEEDS), F32)
    for k in range(K2):
        total = total + jnp.where(position == lanes[k : k + 1, :], 1.0, 0.0)
    return total.astype(BF), start + count


def pick_body(count_ref, neigh_ref, dout_ref, t_ref):
    start = jnp.int32(0)
    lanes = neigh_ref[...]
    d_out = dout_ref[...]
    for s in range(ND):
        picks, start = picks_of(s, start, count_ref, lanes)
        t_ref[s] = dot(picks, d_out).astype(BF)


def rows_body(
    core_ref, own_ref, other_ref, index_ref, ws_ref, wn_ref, wso_ref, wno_ref,
    out_ref, part_ref, table, sums,
):
    core = core_ref[0]
    step = 512
    for c in range(0, NIN, step):
        both = jnp.concatenate([own_ref[:, c : c + step], other_ref[:, c : c + step]], axis=0)
        table[c : c + step, :] = both.astype(F32).T
    for z in range(NZ):
        first = pl.multiple_of((2 * z + core) * OWN, 32)
        out_ref[z, :, 0:PAIR] = table[pl.ds(first, OWN), :].astype(BF)

    def block(b, carry):
        z = b // (OWN // UNROLL)
        base = b * UNROLL + (z + core) * OWN
        for j in range(UNROLL):
            rows = [table[pl.ds(index_ref[k * R1 + base + j], 1), :] for k in range(K1)]
            while len(rows) > 1:
                even = len(rows) // 2 * 2
                rows = [rows[i] + rows[i + 1] for i in range(0, even, 2)] + rows[even:]
            sums[pl.ds(b * UNROLL + j, 1), :] = rows[0]
        return carry

    lax.fori_loop(0, HALF // UNROLL, block, 0)
    w = jnp.concatenate([ws_ref[...], wso_ref[...], wn_ref[...], wno_ref[...]], axis=0)
    for z in range(NZ):
        mean = sums[z * OWN : (z + 1) * OWN, :] * (1.0 / K1)
        out_ref[z, :, PAIR : 2 * PAIR] = mean.astype(BF)
        part_ref[z] = dot(out_ref[z], w).astype(BF)


def split(x):
    high = x.astype(BF)
    return high, (x - high.astype(F32)).astype(BF)


def owner_grads(in_ref, send_ref, seed_ref, dout_ref, w2s_ref, w2n_ref):
    row = lax.broadcasted_iota(I32, (OWN, SEEDS), 0)
    x = jnp.zeros((OWN, HID), F32)
    for q in range(0, ND, 2):
        lanes = jnp.concatenate([send_ref[q : q + 1, :], send_ref[q + 1 : q + 2, :]], axis=1)
        hot = jnp.where(row == lanes, 1.0, 0.0).astype(BF)
        x = x + dot(hot, in_ref[q : q + 2].reshape(2 * SLOTS, HID))
    x = x * (1.0 / K2)
    hot = jnp.where(row == seed_ref[...], 1.0, 0.0).astype(BF)
    d = dot(hot, dout_ref[...]).astype(BF)
    high, low = split(x)
    w2n = w2n_ref[...]
    d_hidden = dot(high, w2n, 1, 1) + dot(low, w2n, 1, 1) + dot(d, w2s_ref[...], 1, 1)
    return high, low, d, d_hidden


def main_body(
    share_ref, in_ref, send_ref, seed_ref, dout_ref, w2s_ref, w2n_ref,
    out_ref, part_ref, dpre_ref,
):
    high, low, d, d_hidden = owner_grads(in_ref, send_ref, seed_ref, dout_ref, w2s_ref, w2n_ref)
    pre = share_ref[0].astype(F32)
    for z in range(1, NZ):
        pre = pre + share_ref[z].astype(F32)
    slope = jnp.exp(jnp.minimum(pre, 0.0))
    hidden = jnp.where(pre > 0, pre, slope - 1.0).astype(BF)
    dpre_ref[...] = (d_hidden * slope).astype(BF)
    g2s = dot(hidden, d, 0, 0).astype(BF)
    g2n = (dot(hidden, high, 0, 0) + dot(hidden, low, 0, 0)).astype(BF)
    for q in range(ND):
        g = g2s if q < 8 else g2n
        for h in range(2):
            piece = g[(q % 8) * 32 : (q % 8) * 32 + 32, h * 128 : (h + 1) * 128]
            out_ref[q, G2 + h * 32 : G2 + h * 32 + 32, :] = piece
    row = lax.broadcasted_iota(I32, (OWN, SEEDS), 0)
    for q in range(0, ND, 2):
        lanes = jnp.concatenate([send_ref[q : q + 1, :], send_ref[q + 1 : q + 2, :]], axis=1)
        hot = jnp.where(row == lanes, 1.0, 0.0).astype(BF)
        listed = dot(hot, hidden, 0, 0).astype(BF)
        for i in range(2):
            for h in range(2):
                piece = listed[i * SLOTS : (i + 1) * SLOTS, h * 128 : (h + 1) * 128]
                out_ref[q + i, h * SLOTS : (h + 1) * SLOTS, :] = piece
    hot = jnp.where(row == seed_ref[...], 1.0, 0.0).astype(BF)
    part_ref[...] = dot(dot(hot, hidden, 0, 0).astype(BF), w2s_ref[...])


def columns_body(chip_ref, rows_ref, *refs):
    keep_ref, give_ref = refs[NZ:]
    chip = chip_ref[0]
    total = jnp.zeros((2 * PAIR, HID), F32)
    for i, offset in enumerate(RING):
        source = jnp.bitwise_and(chip + offset, NZ - 1)
        total = total + dot(rows_ref[source], refs[i][...], 0, 0)
    keep_ref[0:COLS, :] = total[0:COLS]
    keep_ref[COLS:PAIR, :] = total[PAIR : PAIR + COLS]
    give_ref[0:COLS, :] = total[COLS:PAIR]
    give_ref[COLS:PAIR, :] = total[PAIR + COLS :]


def first_sum_body(in_ref, out_ref):
    total = in_ref[0, G2:, :].astype(F32)
    for p in range(1, ND):
        total = total + in_ref[p, G2:, :].astype(F32)
    total = total.astype(BF)
    for f in range(NF):
        out_ref[f] = total


def second_sum_body(keep_ref, got_ref, two_ref, out_ref):
    one = (keep_ref[...] + got_ref[...]).astype(BF)
    two = two_ref[0].astype(F32)
    for f in range(1, NF):
        two = two + two_ref[f].astype(F32)
    two = two.astype(BF)
    for q in range(ND):
        out_ref[q, 0:PAIR, :] = one[:, 0:128]
        out_ref[q, PAIR : 2 * PAIR, :] = one[:, 128:256]
        out_ref[q, 2 * PAIR :, :] = two


def place_body(in_ref, g1s_ref, g1n_ref, g2s_ref, g2n_ref):
    one = in_ref[0, 0 : 2 * PAIR, :].astype(F32)
    for q in range(1, ND):
        one = one + in_ref[q, 0 : 2 * PAIR, :].astype(F32)
    for h in range(2):
        lanes = slice(h * 128, (h + 1) * 128)
        g1s_ref[:, lanes] = one[h * PAIR : h * PAIR + COLS]
        g1n_ref[:, lanes] = one[h * PAIR + COLS : (h + 1) * PAIR]
        for q in range(ND):
            g2 = g2s_ref if q < 8 else g2n_ref
            at = 2 * PAIR + h * 32
            g2[(q % 8) * 32 : (q % 8) * 32 + 32, lanes] = in_ref[q, at : at + 32, :].astype(F32)


def layer_body(count_ref, neigh_ref, in_ref, part_ref, w2n_ref, layer_ref):
    start = jnp.int32(0)
    names = neigh_ref[...]
    total = jnp.zeros((SEEDS, HID), F32)
    for s in range(ND):
        picks, start = picks_of(s, start, count_ref, names)
        rows = [in_ref[s, 0:SLOTS, :], in_ref[s, SLOTS : 2 * SLOTS, :]]
        total = total + dot(picks, jnp.concatenate(rows, axis=1), 0, 0)
    mean_two = (total * (1.0 / K2)).astype(BF)
    layer_ref[...] = (part_ref[...] + dot(mean_two, w2n_ref[...])).astype(BF)


def swap(x, axis, groups=None):
    return lax.all_to_all(
        x, axis, split_axis=0, concat_axis=0, tiled=True, axis_index_groups=groups
    )


def turn(x, step):
    return lax.ppermute(x, "feat", [(i, (i + 2 * step) % NF) for i in range(NF)])


def fetch(x, bit):
    return lax.ppermute(x, "feat", [(i, i ^ bit) for i in range(NF)])


def per_device(
    features, w1_self, w1_neigh, w2_self, w2_neigh, neigh_one, send_rows, recv_count,
    neigh_two, seed_rows, d_out,
):
    f = lax.axis_index("feat")
    core = jnp.bitwise_and(f, 1).reshape(1)
    chip = jnp.right_shift(f, 1).reshape(1)
    chips = [[2 * z + c for z in range(NZ)] for c in range(2)]
    own = features[0]
    other = fetch(own, 1)
    ws_other = fetch(w1_self, 1)
    wn_other = fetch(w1_neigh, 1)

    send = send_rows[0, 0]
    seeds = seed_rows[0]
    grad_out = d_out[0, 0]
    counts = recv_count[:, 0, 0]
    names = neigh_two[0, 0].T
    t_out = call(
        pick_body, "picks", shape((ND, SLOTS, HID), BF), [SMEM, VMEM, VMEM], limit=60, us=5
    )(counts, names, grad_out)
    t_in = swap(t_out, "dom")

    rows = shape((NZ, OWN, 2 * PAIR), BF)
    rows, share = call(
        rows_body,
        "node_rows",
        (rows, rows),
        [SMEM, VMEM, VMEM, SMEM] + [VMEM] * 4,
        [pltpu.VMEM((NIN, PAIR), F32), pltpu.VMEM((HALF, PAIR), F32)],
        limit=60,
        us=22,
    )(core, own, other, neigh_one.reshape(-1), w1_self, w1_neigh, ws_other, wn_other)
    share = swap(share, "feat", chips)

    to_dom, part, d_pre = call(
        main_body,
        "project",
        (
            shape((ND, G2 + 64, 128), BF),
            shape((SEEDS, HID), F32),
            shape((OWN, HID), BF),
        ),
        [VMEM] * 7,
        us=4,
    )(share, t_in, send, seeds, grad_out, w2_self, w2_neigh)

    ring = {0: d_pre}
    for i in range(1, 4):
        ring[-i] = turn(ring[1 - i], 1)
        ring[i] = turn(ring[i - 1], -1)
    ring[-4] = turn(ring[-3], 1)
    from_dom = swap(to_dom, "dom")

    two = call(first_sum_body, "sum_dom", shape((NF, 64, 128), BF), [VMEM])(from_dom)
    two, ring[-4] = lax.optimization_barrier((two, ring[-4]))
    two = swap(two, "feat")
    keep, give = call(
        columns_body,
        "columns",
        (shape((PAIR, HID), F32), shape((PAIR, HID), F32)),
        [SMEM] + [VMEM] * (1 + NZ),
        us=2,
    )(chip, rows, *[ring[i] for i in RING])
    got = fetch(give, 1)
    layer_out = call(
        layer_body,
        "layer_two",
        shape((SEEDS, HID), BF),
        [SMEM] + [VMEM] * 4,
        limit=60,
        us=5,
    )(counts, names, from_dom, part, w2_neigh)
    done = call(
        second_sum_body, "sum_feat", shape((ND, 2 * PAIR + 64, 128), BF), [VMEM] * 3, limit=60
    )(keep, got, two)
    done = swap(done, "dom")
    first = shape((COLS, HID), F32)
    second = shape((HID, HID), F32)
    grads = call(place_body, "place", (first, first, second, second), [VMEM])(done)
    return (layer_out[None, None], *grads)


def solution(mesh):
    return jax.shard_map(
        per_device,
        mesh=mesh,
        in_specs=(
            P("dom", "feat", None),
            P("feat", None),
            P("feat", None),
            P(),
            P(),
            P("dom", None, None),
            P("dom", "feat", None, None),
            P(None, "feat", "dom"),
            P("dom", "feat", None, None),
            P("dom", "feat", None),
            P("dom", "feat", None, None),
        ),
        out_specs=(P("dom", "feat", None, None), P("feat", None), P("feat", None), P(), P()),
        check_vma=False,
    )
```

```python
import jax
import jax.numpy as jnp
from jax import lax
from jax.experimental import pallas as pl
from jax.experimental.pallas import tpu as pltpu
from jax.sharding import PartitionSpec as P

BF = jnp.bfloat16
F32 = jnp.float32
I32 = jnp.int32
NF = 16
ND = 16
NZ = 8
COLS = 64
PAIR = 128
NIN = 9216
R1 = 4608
OWN = 288
HALF = R1 // 2
K1 = 10
K2 = 15
SEEDS = 256
SLOTS = 128
HID = 256
UNROLL = 32
G2 = 256
RING = (0, -1, 1, -2, 2, -3, 3, -4)
VMEM = pl.BlockSpec(memory_space=pltpu.VMEM)
SMEM = pl.BlockSpec(memory_space=pltpu.SMEM)


def call(body, name, outs, ins, scratch=(), limit=16, us=1):
    return pl.pallas_call(
        body,
        name=name,
        out_shape=outs,
        in_specs=ins,
        out_specs=jax.tree.map(lambda _: VMEM, outs),
        scratch_shapes=list(scratch),
        compiler_params=pltpu.CompilerParams(vmem_limit_bytes=limit << 20),
        cost_estimate=pl.CostEstimate(flops=us * 10**9, transcendentals=0, bytes_accessed=us * 10**6),
    )


def shape(dims, dtype):
    return jax.ShapeDtypeStruct(dims, dtype)


def dot(a, b, ca=1, cb=0):
    return lax.dot_general(a, b, (((ca,), (cb,)), ((), ())), preferred_element_type=F32)


def picks_by_source(count_ref, neigh_ref, hot):
    names = neigh_ref[...].T
    source = jnp.zeros(names.shape, I32)
    base = jnp.zeros(names.shape, I32)
    start = jnp.int32(0)
    for s in range(1, ND):
        start = start + count_ref[s - 1]
        later = names >= start
        source = jnp.where(later, s, source)
        base = jnp.where(later, start, base)
    slot = names - base
    row = lax.broadcasted_iota(I32, (SLOTS, SEEDS), 0)
    for k in range(K2):
        hot[k] = jnp.where(row == slot[k : k + 1, :], 1.0, 0.0).astype(BF)
    for s in range(ND):
        here = jnp.where(source == s, 1.0, 0.0).astype(BF)
        total = jnp.zeros((SLOTS, SEEDS), BF)
        for k in range(K2):
            total = total + hot[k] * here[k : k + 1, :]
        yield s, total


def pick_body(count_ref, neigh_ref, dout_ref, t_ref, hot):
    d_out = dout_ref[...]
    for s, picks in picks_by_source(count_ref, neigh_ref, hot):
        t_ref[s] = dot(picks, d_out).astype(BF)


def rows_body(
    core_ref, own_ref, other_ref, index_ref, ws_ref, wn_ref, wso_ref, wno_ref,
    out_ref, part_ref, table, sums,
):
    core = core_ref[0]
    step = 512
    for c in range(0, NIN, step):
        both = jnp.concatenate([own_ref[:, c : c + step], other_ref[:, c : c + step]], axis=0)
        table[c : c + step, :] = both.astype(F32).T
    for z in range(NZ):
        first = pl.multiple_of((2 * z + core) * OWN, 32)
        out_ref[z, :, 0:PAIR] = table[pl.ds(first, OWN), :].astype(BF)

    def block(b, carry):
        z = b // (OWN // UNROLL)
        base = b * UNROLL + (z + core) * OWN
        for j in range(UNROLL):
            rows = [table[pl.ds(index_ref[k * R1 + base + j], 1), :] for k in range(K1)]
            while len(rows) > 1:
                even = len(rows) // 2 * 2
                rows = [rows[i] + rows[i + 1] for i in range(0, even, 2)] + rows[even:]
            sums[pl.ds(b * UNROLL + j, 1), :] = rows[0]
        return carry

    lax.fori_loop(0, HALF // UNROLL, block, 0)
    w = jnp.concatenate([ws_ref[...], wso_ref[...], wn_ref[...], wno_ref[...]], axis=0)
    for z in range(NZ):
        mean = sums[z * OWN : (z + 1) * OWN, :] * (1.0 / K1)
        out_ref[z, :, PAIR : 2 * PAIR] = mean.astype(BF)
        part_ref[z] = dot(out_ref[z], w).astype(BF)


def split(x):
    high = x.astype(BF)
    return high, (x - high.astype(F32)).astype(BF)


def owner_grads(in_ref, send_ref, seed_ref, dout_ref, w2s_ref, w2n_ref):
    row = lax.broadcasted_iota(I32, (OWN, SEEDS), 0)
    x = jnp.zeros((OWN, HID), F32)
    for q in range(0, ND, 2):
        lanes = jnp.concatenate([send_ref[q : q + 1, :], send_ref[q + 1 : q + 2, :]], axis=1)
        hot = jnp.where(row == lanes, 1.0, 0.0).astype(BF)
        x = x + dot(hot, in_ref[q : q + 2].reshape(2 * SLOTS, HID))
    x = x * (1.0 / K2)
    hot = jnp.where(row == seed_ref[...], 1.0, 0.0).astype(BF)
    d = dot(hot, dout_ref[...]).astype(BF)
    high, low = split(x)
    w2n = w2n_ref[...]
    d_hidden = dot(high, w2n, 1, 1) + dot(low, w2n, 1, 1) + dot(d, w2s_ref[...], 1, 1)
    return high, low, d, d_hidden


def main_body(
    share_ref, in_ref, send_ref, seed_ref, dout_ref, w2s_ref, w2n_ref,
    out_ref, part_ref, dpre_ref,
):
    high, low, d, d_hidden = owner_grads(in_ref, send_ref, seed_ref, dout_ref, w2s_ref, w2n_ref)
    pre = share_ref[0].astype(F32)
    for z in range(1, NZ):
        pre = pre + share_ref[z].astype(F32)
    slope = jnp.exp(jnp.minimum(pre, 0.0))
    hidden = jnp.where(pre > 0, pre, slope - 1.0).astype(BF)
    dpre_ref[...] = (d_hidden * slope).astype(BF)
    g2s = dot(hidden, d, 0, 0).astype(BF)
    g2n = (dot(hidden, high, 0, 0) + dot(hidden, low, 0, 0)).astype(BF)
    for q in range(ND):
        g = g2s if q < 8 else g2n
        for h in range(2):
            piece = g[(q % 8) * 32 : (q % 8) * 32 + 32, h * 128 : (h + 1) * 128]
            out_ref[q, G2 + h * 32 : G2 + h * 32 + 32, :] = piece
    row = lax.broadcasted_iota(I32, (OWN, SEEDS), 0)
    for q in range(0, ND, 2):
        lanes = jnp.concatenate([send_ref[q : q + 1, :], send_ref[q + 1 : q + 2, :]], axis=1)
        hot = jnp.where(row == lanes, 1.0, 0.0).astype(BF)
        listed = dot(hot, hidden, 0, 0).astype(BF)
        for i in range(2):
            for h in range(2):
                piece = listed[i * SLOTS : (i + 1) * SLOTS, h * 128 : (h + 1) * 128]
                out_ref[q + i, h * SLOTS : (h + 1) * SLOTS, :] = piece
    hot = jnp.where(row == seed_ref[...], 1.0, 0.0).astype(BF)
    part_ref[...] = dot(dot(hot, hidden, 0, 0).astype(BF), w2s_ref[...])


def columns_body(chip_ref, rows_ref, *refs):
    keep_ref, give_ref = refs[NZ:]
    chip = chip_ref[0]
    total = jnp.zeros((2 * PAIR, HID), F32)
    for i, offset in enumerate(RING):
        source = jnp.bitwise_and(chip + offset, NZ - 1)
        total = total + dot(rows_ref[source], refs[i][...], 0, 0)
    keep_ref[0:COLS, :] = total[0:COLS]
    keep_ref[COLS:PAIR, :] = total[PAIR : PAIR + COLS]
    give_ref[0:COLS, :] = total[COLS:PAIR]
    give_ref[COLS:PAIR, :] = total[PAIR + COLS :]


def first_sum_body(in_ref, out_ref):
    total = in_ref[0, G2:, :].astype(F32)
    for p in range(1, ND):
        total = total + in_ref[p, G2:, :].astype(F32)
    total = total.astype(BF)
    for f in range(NF):
        out_ref[f] = total


def second_sum_body(keep_ref, got_ref, two_ref, out_ref):
    one = (keep_ref[...] + got_ref[...]).astype(BF)
    two = two_ref[0].astype(F32)
    for f in range(1, NF):
        two = two + two_ref[f].astype(F32)
    two = two.astype(BF)
    for q in range(ND):
        out_ref[q, 0:PAIR, :] = one[:, 0:128]
        out_ref[q, PAIR : 2 * PAIR, :] = one[:, 128:256]
        out_ref[q, 2 * PAIR :, :] = two


def place_body(in_ref, g1s_ref, g1n_ref, g2s_ref, g2n_ref):
    one = in_ref[0, 0 : 2 * PAIR, :].astype(F32)
    for q in range(1, ND):
        one = one + in_ref[q, 0 : 2 * PAIR, :].astype(F32)
    for h in range(2):
        lanes = slice(h * 128, (h + 1) * 128)
        g1s_ref[:, lanes] = one[h * PAIR : h * PAIR + COLS]
        g1n_ref[:, lanes] = one[h * PAIR + COLS : (h + 1) * PAIR]
        for q in range(ND):
            g2 = g2s_ref if q < 8 else g2n_ref
            at = 2 * PAIR + h * 32
            g2[(q % 8) * 32 : (q % 8) * 32 + 32, lanes] = in_ref[q, at : at + 32, :].astype(F32)


def layer_body(count_ref, neigh_ref, in_ref, part_ref, w2n_ref, layer_ref, hot):
    total = jnp.zeros((SEEDS, HID), F32)
    for s, picks in picks_by_source(count_ref, neigh_ref, hot):
        rows = [in_ref[s, 0:SLOTS, :], in_ref[s, SLOTS : 2 * SLOTS, :]]
        total = total + dot(picks, jnp.concatenate(rows, axis=1), 0, 0)
    mean_two = (total * (1.0 / K2)).astype(BF)
    layer_ref[...] = (part_ref[...] + dot(mean_two, w2n_ref[...])).astype(BF)


def swap(x, axis, groups=None):
    return lax.all_to_all(
        x, axis, split_axis=0, concat_axis=0, tiled=True, axis_index_groups=groups
    )


def turn(x, step):
    return lax.ppermute(x, "feat", [(i, (i + 2 * step) % NF) for i in range(NF)])


def fetch(x, bit):
    return lax.ppermute(x, "feat", [(i, i ^ bit) for i in range(NF)])


def per_device(
    features, w1_self, w1_neigh, w2_self, w2_neigh, neigh_one, send_rows, recv_count,
    neigh_two, seed_rows, d_out,
):
    f = lax.axis_index("feat")
    core = jnp.bitwise_and(f, 1).reshape(1)
    chip = jnp.right_shift(f, 1).reshape(1)
    chips = [[2 * z + c for z in range(NZ)] for c in range(2)]
    own = features[0]
    other = fetch(own, 1)
    ws_other = fetch(w1_self, 1)
    wn_other = fetch(w1_neigh, 1)

    send = send_rows[0, 0]
    seeds = seed_rows[0]
    grad_out = d_out[0, 0]
    counts = recv_count[:, 0, 0]
    names = neigh_two[0, 0]
    hot = [pltpu.VMEM((K2, SLOTS, SEEDS), BF)]
    t_out = call(
        pick_body, "picks", shape((ND, SLOTS, HID), BF), [SMEM, VMEM, VMEM], hot, limit=60, us=4
    )(counts, names, grad_out)
    t_in = swap(t_out, "dom")

    rows = shape((NZ, OWN, 2 * PAIR), BF)
    rows, share = call(
        rows_body,
        "node_rows",
        (rows, rows),
        [SMEM, VMEM, VMEM, SMEM] + [VMEM] * 4,
        [pltpu.VMEM((NIN, PAIR), F32), pltpu.VMEM((HALF, PAIR), F32)],
        limit=60,
        us=22,
    )(core, own, other, neigh_one.reshape(-1), w1_self, w1_neigh, ws_other, wn_other)
    share = swap(share, "feat", chips)

    to_dom, part, d_pre = call(
        main_body,
        "project",
        (
            shape((ND, G2 + 64, 128), BF),
            shape((SEEDS, HID), F32),
            shape((OWN, HID), BF),
        ),
        [VMEM] * 7,
        us=4,
    )(share, t_in, send, seeds, grad_out, w2_self, w2_neigh)

    from_dom = swap(to_dom, "dom")
    ring = {0: d_pre}
    for i in range(1, 4):
        ring[-i], ring[i] = lax.optimization_barrier((turn(ring[1 - i], 1), turn(ring[i - 1], -1)))
    from_dom, last = lax.optimization_barrier((from_dom, ring[-3]))
    ring[-4] = turn(last, 1)
    two = call(first_sum_body, "sum_dom", shape((NF, 64, 128), BF), [VMEM])(from_dom)
    two, ring[-3] = lax.optimization_barrier((two, ring[-3]))
    two = swap(two, "feat")
    keep, give = call(
        columns_body,
        "columns",
        (shape((PAIR, HID), F32), shape((PAIR, HID), F32)),
        [SMEM] + [VMEM] * (1 + NZ),
        us=2,
    )(chip, rows, *[ring[i] for i in RING])
    got = fetch(give, 1)
    layer_out = call(
        layer_body,
        "layer_two",
        shape((SEEDS, HID), BF),
        [SMEM] + [VMEM] * 4,
        hot,
        limit=60,
        us=5,
    )(counts, names, from_dom, part, w2_neigh)
    done = call(
        second_sum_body, "sum_feat", shape((ND, 2 * PAIR + 64, 128), BF), [VMEM] * 3, limit=60
    )(keep, got, two)
    done = swap(done, "dom")
    first = shape((COLS, HID), F32)
    second = shape((HID, HID), F32)
    grads = call(place_body, "place", (first, first, second, second), [VMEM])(done)
    return (layer_out[None, None], *grads)


def solution(mesh):
    return jax.shard_map(
        per_device,
        mesh=mesh,
        in_specs=(
            P("dom", "feat", None),
            P("feat", None),
            P("feat", None),
            P(),
            P(),
            P("dom", None, None),
            P("dom", "feat", None, None),
            P(None, "feat", "dom"),
            P("dom", "feat", None, None),
            P("dom", "feat", None),
            P("dom", "feat", None, None),
        ),
        out_specs=(P("dom", "feat", None, None), P("feat", None), P("feat", None), P(), P()),
        check_vma=False,
    )
```

```python
import jax
import jax.numpy as jnp
from jax import lax
from jax.experimental import pallas as pl
from jax.experimental.pallas import tpu as pltpu
from jax.sharding import PartitionSpec as P

BF = jnp.bfloat16
F32 = jnp.float32
I32 = jnp.int32
NF = 16
ND = 16
NZ = 8
COLS = 64
PAIR = 128
NIN = 9216
R1 = 4608
OWN = 288
HALF = R1 // 2
K1 = 10
K2 = 15
SEEDS = 256
SLOTS = 128
HID = 256
UNROLL = 32
G2 = 256
RING = (0, -1, 1, -2, 2, -3, 3, -4)
VMEM = pl.BlockSpec(memory_space=pltpu.VMEM)
SMEM = pl.BlockSpec(memory_space=pltpu.SMEM)


def call(body, name, outs, ins, scratch=(), limit=16, us=1):
    return pl.pallas_call(
        body,
        name=name,
        out_shape=outs,
        in_specs=ins,
        out_specs=jax.tree.map(lambda _: VMEM, outs),
        scratch_shapes=list(scratch),
        compiler_params=pltpu.CompilerParams(vmem_limit_bytes=limit << 20),
        cost_estimate=pl.CostEstimate(flops=us * 10**9, transcendentals=0, bytes_accessed=us * 10**6),
    )


def shape(dims, dtype):
    return jax.ShapeDtypeStruct(dims, dtype)


def dot(a, b, ca=1, cb=0):
    return lax.dot_general(a, b, (((ca,), (cb,)), ((), ())), preferred_element_type=F32)


def picks_by_source(count_ref, neigh_ref, hot):
    names = neigh_ref[...].reshape(K2, SEEDS)
    source = jnp.zeros(names.shape, I32)
    base = jnp.zeros(names.shape, I32)
    start = jnp.int32(0)
    for s in range(1, ND):
        start = start + count_ref[s - 1]
        later = names >= start
        source = jnp.where(later, s, source)
        base = jnp.where(later, start, base)
    slot = names - base
    row = lax.broadcasted_iota(I32, (SLOTS, SEEDS), 0)
    for k in range(K2):
        hot[k] = jnp.where(row == slot[k : k + 1, :], 1.0, 0.0).astype(BF)
    for s in range(ND):
        here = jnp.where(source == s, 1.0, 0.0).astype(BF)
        total = jnp.zeros((SLOTS, SEEDS), BF)
        for k in range(K2):
            total = total + hot[k] * here[k : k + 1, :]
        yield s, total


def pick_body(count_ref, neigh_ref, dout_ref, t_ref, hot):
    d_out = dout_ref[...]
    for s, picks in picks_by_source(count_ref, neigh_ref, hot):
        t_ref[s] = dot(picks, d_out).astype(BF)


def rows_body(
    core_ref, own_ref, other_ref, index_ref, ws_ref, wn_ref, wso_ref, wno_ref,
    out_ref, part_ref, table, sums,
):
    core = core_ref[0]
    step = 512
    for c in range(0, NIN, step):
        both = jnp.concatenate([own_ref[:, c : c + step], other_ref[:, c : c + step]], axis=0)
        table[c : c + step, :] = both.astype(F32).T
    for z in range(NZ):
        first = pl.multiple_of((2 * z + core) * OWN, 32)
        out_ref[z, :, 0:PAIR] = table[pl.ds(first, OWN), :].astype(BF)

    def block(b, carry):
        z = b // (OWN // UNROLL)
        base = b * UNROLL + (z + core) * OWN
        for j in range(UNROLL):
            rows = [table[pl.ds(index_ref[k * R1 + base + j], 1), :] for k in range(K1)]
            while len(rows) > 1:
                even = len(rows) // 2 * 2
                rows = [rows[i] + rows[i + 1] for i in range(0, even, 2)] + rows[even:]
            sums[pl.ds(b * UNROLL + j, 1), :] = rows[0]
        return carry

    lax.fori_loop(0, HALF // UNROLL, block, 0)
    w = jnp.concatenate([ws_ref[...], wso_ref[...], wn_ref[...], wno_ref[...]], axis=0)
    for z in range(NZ):
        mean = sums[z * OWN : (z + 1) * OWN, :] * (1.0 / K1)
        out_ref[z, :, PAIR : 2 * PAIR] = mean.astype(BF)
        part_ref[z] = dot(out_ref[z], w).astype(BF)


def split(x):
    high = x.astype(BF)
    return high, (x - high.astype(F32)).astype(BF)


def owner_grads(in_ref, send_ref, seed_ref, dout_ref, w2s_ref, w2n_ref):
    row = lax.broadcasted_iota(I32, (OWN, SEEDS), 0)
    x = jnp.zeros((OWN, HID), F32)
    for q in range(0, ND, 2):
        lanes = jnp.concatenate([send_ref[q : q + 1, :], send_ref[q + 1 : q + 2, :]], axis=1)
        hot = jnp.where(row == lanes, 1.0, 0.0).astype(BF)
        x = x + dot(hot, in_ref[q : q + 2].reshape(2 * SLOTS, HID))
    x = x * (1.0 / K2)
    hot = jnp.where(row == seed_ref[...], 1.0, 0.0).astype(BF)
    d = dot(hot, dout_ref[...]).astype(BF)
    high, low = split(x)
    w2n = w2n_ref[...]
    d_hidden = dot(high, w2n, 1, 1) + dot(low, w2n, 1, 1) + dot(d, w2s_ref[...], 1, 1)
    return high, low, d, d_hidden


def main_body(
    share_ref, in_ref, send_ref, seed_ref, dout_ref, w2s_ref, w2n_ref,
    out_ref, part_ref, dpre_ref,
):
    high, low, d, d_hidden = owner_grads(in_ref, send_ref, seed_ref, dout_ref, w2s_ref, w2n_ref)
    pre = share_ref[0].astype(F32)
    for z in range(1, NZ):
        pre = pre + share_ref[z].astype(F32)
    slope = jnp.exp(jnp.minimum(pre, 0.0))
    hidden = jnp.where(pre > 0, pre, slope - 1.0).astype(BF)
    dpre_ref[...] = (d_hidden * slope).astype(BF)
    g2s = dot(hidden, d, 0, 0).astype(BF)
    g2n = (dot(hidden, high, 0, 0) + dot(hidden, low, 0, 0)).astype(BF)
    for q in range(ND):
        g = g2s if q < 8 else g2n
        for h in range(2):
            piece = g[(q % 8) * 32 : (q % 8) * 32 + 32, h * 128 : (h + 1) * 128]
            out_ref[q, G2 + h * 32 : G2 + h * 32 + 32, :] = piece
    row = lax.broadcasted_iota(I32, (OWN, SEEDS), 0)
    for q in range(0, ND, 2):
        lanes = jnp.concatenate([send_ref[q : q + 1, :], send_ref[q + 1 : q + 2, :]], axis=1)
        hot = jnp.where(row == lanes, 1.0, 0.0).astype(BF)
        listed = dot(hot, hidden, 0, 0).astype(BF)
        for i in range(2):
            for h in range(2):
                piece = listed[i * SLOTS : (i + 1) * SLOTS, h * 128 : (h + 1) * 128]
                out_ref[q + i, h * SLOTS : (h + 1) * SLOTS, :] = piece
    hot = jnp.where(row == seed_ref[...], 1.0, 0.0).astype(BF)
    part_ref[...] = dot(dot(hot, hidden, 0, 0).astype(BF), w2s_ref[...])


def columns_body(chip_ref, rows_ref, *refs):
    keep_ref, give_ref = refs[NZ:]
    chip = chip_ref[0]
    total = jnp.zeros((2 * PAIR, HID), F32)
    for i, offset in enumerate(RING):
        source = jnp.bitwise_and(chip + offset, NZ - 1)
        total = total + dot(rows_ref[source], refs[i][...], 0, 0)
    keep_ref[0:COLS, :] = total[0:COLS]
    keep_ref[COLS:PAIR, :] = total[PAIR : PAIR + COLS]
    give_ref[0:COLS, :] = total[COLS:PAIR]
    give_ref[COLS:PAIR, :] = total[PAIR + COLS :]


def first_sum_body(in_ref, out_ref):
    total = in_ref[0, G2:, :].astype(F32)
    for p in range(1, ND):
        total = total + in_ref[p, G2:, :].astype(F32)
    total = total.astype(BF)
    for f in range(NF):
        out_ref[f] = total


def second_sum_body(two_ref, out_ref):
    two = two_ref[0].astype(F32)
    for f in range(1, NF):
        two = two + two_ref[f].astype(F32)
    two = two.astype(BF)
    for q in range(ND):
        out_ref[q] = two


def place_body(in_ref, g2s_ref, g2n_ref):
    for q in range(ND):
        g2 = g2s_ref if q < 8 else g2n_ref
        for h in range(2):
            piece = in_ref[q, h * 32 : h * 32 + 32, :].astype(F32)
            g2[(q % 8) * 32 : (q % 8) * 32 + 32, h * 128 : (h + 1) * 128] = piece


def layer_body(count_ref, neigh_ref, in_ref, part_ref, w2n_ref, layer_ref, hot):
    total = jnp.zeros((SEEDS, HID), F32)
    for s, picks in picks_by_source(count_ref, neigh_ref, hot):
        rows = [in_ref[s, 0:SLOTS, :], in_ref[s, SLOTS : 2 * SLOTS, :]]
        total = total + dot(picks, jnp.concatenate(rows, axis=1), 0, 0)
    mean_two = (total * (1.0 / K2)).astype(BF)
    layer_ref[...] = (part_ref[...] + dot(mean_two, w2n_ref[...])).astype(BF)


def swap(x, axis, groups=None):
    return lax.all_to_all(
        x, axis, split_axis=0, concat_axis=0, tiled=True, axis_index_groups=groups
    )


def turn(x, step):
    return lax.ppermute(x, "feat", [(i, (i + 2 * step) % NF) for i in range(NF)])


def along(x, step):
    pairs = [(i, (i + step) % ND if step % 4 == 0 else i // 4 * 4 + (i + step) % 4) for i in range(ND)]
    return lax.ppermute(x, "dom", pairs)


def fetch(x, bit):
    return lax.ppermute(x, "feat", [(i, i ^ bit) for i in range(NF)])


def per_device(
    features, w1_self, w1_neigh, w2_self, w2_neigh, neigh_one, send_rows, recv_count,
    neigh_two, seed_rows, d_out,
):
    f = lax.axis_index("feat")
    core = jnp.bitwise_and(f, 1).reshape(1)
    chip = jnp.right_shift(f, 1).reshape(1)
    chips = [[2 * z + c for z in range(NZ)] for c in range(2)]
    own = features[0]
    other = fetch(own, 1)
    ws_other = fetch(w1_self, 1)
    wn_other = fetch(w1_neigh, 1)

    send = send_rows[0, 0]
    seeds = seed_rows[0]
    grad_out = d_out[0, 0]
    counts = recv_count[:, 0, 0]
    names = neigh_two[0].transpose(2, 0, 1)
    hot = [pltpu.VMEM((K2, SLOTS, SEEDS), BF)]
    t_out = call(
        pick_body, "picks", shape((ND, SLOTS, HID), BF), [SMEM, VMEM, VMEM], hot, limit=60, us=4
    )(counts, names, grad_out)
    t_in = swap(t_out, "dom")

    rows = shape((NZ, OWN, 2 * PAIR), BF)
    rows, share = call(
        rows_body,
        "node_rows",
        (rows, rows),
        [SMEM, VMEM, VMEM, SMEM] + [VMEM] * 4,
        [pltpu.VMEM((NIN, PAIR), F32), pltpu.VMEM((HALF, PAIR), F32)],
        limit=60,
        us=22,
    )(core, own, other, neigh_one.reshape(-1), w1_self, w1_neigh, ws_other, wn_other)
    share = swap(share, "feat", chips)

    to_dom, part, d_pre = call(
        main_body,
        "project",
        (
            shape((ND, G2 + 64, 128), BF),
            shape((SEEDS, HID), F32),
            shape((OWN, HID), BF),
        ),
        [VMEM] * 7,
        us=4,
    )(share, t_in, send, seeds, grad_out, w2_self, w2_neigh)

    from_dom = swap(to_dom, "dom")
    ring = {0: d_pre}
    for i in range(1, 4):
        ring[-i], ring[i] = lax.optimization_barrier((turn(ring[1 - i], 1), turn(ring[i - 1], -1)))
    from_dom, last = lax.optimization_barrier((from_dom, ring[-3]))
    ring[-4] = turn(last, 1)
    two = call(first_sum_body, "sum_dom", shape((NF, 64, 128), BF), [VMEM])(from_dom)
    two, ring[-4] = lax.optimization_barrier((two, ring[-4]))
    two = swap(two, "feat")
    keep, give = call(
        columns_body,
        "columns",
        (shape((PAIR, HID), F32), shape((PAIR, HID), F32)),
        [SMEM] + [VMEM] * (1 + NZ),
        us=2,
    )(chip, rows, *[ring[i] for i in RING])
    one = keep + fetch(give, 1)
    one = one + sum(along(one, 4 * i) for i in range(1, 4))
    one = one + sum(along(one, i) for i in range(1, 4))
    layer_out = call(
        layer_body,
        "layer_two",
        shape((SEEDS, HID), BF),
        [SMEM] + [VMEM] * 4,
        hot,
        us=5,
    )(counts, names, from_dom, part, w2_neigh)
    done = call(second_sum_body, "sum_feat", shape((ND, 64, 128), BF), [VMEM], limit=60)(two)
    done = swap(done, "dom")
    second = shape((HID, HID), F32)
    two_self, two_neigh = call(place_body, "place", (second, second), [VMEM])(done)
    return (layer_out[None, None], one[:COLS], one[COLS:], two_self, two_neigh)


def solution(mesh):
    return jax.shard_map(
        per_device,
        mesh=mesh,
        in_specs=(
            P("dom", "feat", None),
            P("feat", None),
            P("feat", None),
            P(),
            P(),
            P("dom", None, None),
            P("dom", "feat", None, None),
            P(None, "feat", "dom"),
            P("dom", "feat", None, None),
            P("dom", "feat", None),
            P("dom", "feat", None, None),
        ),
        out_specs=(P("dom", "feat", None, None), P("feat", None), P("feat", None), P(), P()),
        check_vma=False,
    )
```

```python
import jax
import jax.numpy as jnp
from jax import lax
from jax.experimental import pallas as pl
from jax.experimental.pallas import tpu as pltpu
from jax.sharding import PartitionSpec as P

BF = jnp.bfloat16
F32 = jnp.float32
I32 = jnp.int32
NF = 16
ND = 16
NZ = 8
COLS = 64
PAIR = 128
NIN = 9216
R1 = 4608
OWN = 288
HALF = R1 // 2
K1 = 10
K2 = 15
SEEDS = 256
SLOTS = 128
HID = 256
UNROLL = 32
G2 = 256
RING = (0, -1, 1, -2, 2, -3, 3, -4)
VMEM = pl.BlockSpec(memory_space=pltpu.VMEM)
SMEM = pl.BlockSpec(memory_space=pltpu.SMEM)


def call(body, name, outs, ins, scratch=(), limit=16, us=1):
    return pl.pallas_call(
        body,
        name=name,
        out_shape=outs,
        in_specs=ins,
        out_specs=jax.tree.map(lambda _: VMEM, outs),
        scratch_shapes=list(scratch),
        compiler_params=pltpu.CompilerParams(vmem_limit_bytes=limit << 20),
        cost_estimate=pl.CostEstimate(flops=us * 10**9, transcendentals=0, bytes_accessed=us * 10**6),
    )


def shape(dims, dtype):
    return jax.ShapeDtypeStruct(dims, dtype)


def dot(a, b, ca=1, cb=0):
    return lax.dot_general(a, b, (((ca,), (cb,)), ((), ())), preferred_element_type=F32)


def picks_by_source(count_ref, neigh_ref, hot):
    names = neigh_ref[...].reshape(K2, SEEDS)
    source = jnp.zeros(names.shape, I32)
    base = jnp.zeros(names.shape, I32)
    start = jnp.int32(0)
    for s in range(1, ND):
        start = start + count_ref[s - 1]
        later = names >= start
        source = jnp.where(later, s, source)
        base = jnp.where(later, start, base)
    slot = names - base
    row = lax.broadcasted_iota(I32, (SLOTS, SEEDS), 0)
    for k in range(K2):
        hot[k] = jnp.where(row == slot[k : k + 1, :], 1.0, 0.0).astype(BF)
    for s in range(ND):
        here = jnp.where(source == s, 1.0, 0.0).astype(BF)
        total = jnp.zeros((SLOTS, SEEDS), BF)
        for k in range(K2):
            total = total + hot[k] * here[k : k + 1, :]
        yield s, total


def pick_body(count_ref, neigh_ref, dout_ref, t_ref, hot):
    d_out = dout_ref[...]
    for s, picks in picks_by_source(count_ref, neigh_ref, hot):
        t_ref[s] = dot(picks, d_out).astype(BF)


def rows_body(
    core_ref, own_ref, other_ref, index_ref, ws_ref, wn_ref, wso_ref, wno_ref,
    out_ref, part_ref, table, sums,
):
    core = core_ref[0]
    step = 512
    for c in range(0, NIN, step):
        both = jnp.concatenate([own_ref[:, c : c + step], other_ref[:, c : c + step]], axis=0)
        table[c : c + step, :] = both.astype(F32).T
    for z in range(NZ):
        first = pl.multiple_of((2 * z + core) * OWN, 32)
        out_ref[z, :, 0:PAIR] = table[pl.ds(first, OWN), :].astype(BF)

    def block(b, carry):
        z = b // (OWN // UNROLL)
        base = b * UNROLL + (z + core) * OWN
        for j in range(UNROLL):
            rows = [table[pl.ds(index_ref[k * R1 + base + j], 1), :] for k in range(K1)]
            while len(rows) > 1:
                even = len(rows) // 2 * 2
                rows = [rows[i] + rows[i + 1] for i in range(0, even, 2)] + rows[even:]
            sums[pl.ds(b * UNROLL + j, 1), :] = rows[0]
        return carry

    lax.fori_loop(0, HALF // UNROLL, block, 0)
    w = jnp.concatenate([ws_ref[...], wso_ref[...], wn_ref[...], wno_ref[...]], axis=0)
    for z in range(NZ):
        mean = sums[z * OWN : (z + 1) * OWN, :] * (1.0 / K1)
        out_ref[z, :, PAIR : 2 * PAIR] = mean.astype(BF)
        part_ref[z] = dot(out_ref[z], w).astype(BF)


def split(x):
    high = x.astype(BF)
    return high, (x - high.astype(F32)).astype(BF)


def owner_grads(in_ref, send_ref, seed_ref, dout_ref, w2s_ref, w2n_ref):
    row = lax.broadcasted_iota(I32, (OWN, SEEDS), 0)
    x = jnp.zeros((OWN, HID), F32)
    for q in range(0, ND, 2):
        lanes = jnp.concatenate([send_ref[q : q + 1, :], send_ref[q + 1 : q + 2, :]], axis=1)
        hot = jnp.where(row == lanes, 1.0, 0.0).astype(BF)
        x = x + dot(hot, in_ref[q : q + 2].reshape(2 * SLOTS, HID))
    x = x * (1.0 / K2)
    hot = jnp.where(row == seed_ref[...], 1.0, 0.0).astype(BF)
    d = dot(hot, dout_ref[...]).astype(BF)
    high, low = split(x)
    w2n = w2n_ref[...]
    d_hidden = dot(high, w2n, 1, 1) + dot(low, w2n, 1, 1) + dot(d, w2s_ref[...], 1, 1)
    return high, low, d, d_hidden


def main_body(
    share_ref, in_ref, send_ref, seed_ref, dout_ref, w2s_ref, w2n_ref,
    out_ref, part_ref, dpre_ref,
):
    high, low, d, d_hidden = owner_grads(in_ref, send_ref, seed_ref, dout_ref, w2s_ref, w2n_ref)
    pre = share_ref[0].astype(F32)
    for z in range(1, NZ):
        pre = pre + share_ref[z].astype(F32)
    slope = jnp.exp(jnp.minimum(pre, 0.0))
    hidden = jnp.where(pre > 0, pre, slope - 1.0).astype(BF)
    dpre_ref[...] = (d_hidden * slope).astype(BF)
    g2s = dot(hidden, d, 0, 0).astype(BF)
    g2n = (dot(hidden, high, 0, 0) + dot(hidden, low, 0, 0)).astype(BF)
    for q in range(ND):
        g = g2s if q < 8 else g2n
        for h in range(2):
            piece = g[(q % 8) * 32 : (q % 8) * 32 + 32, h * 128 : (h + 1) * 128]
            out_ref[q, G2 + h * 32 : G2 + h * 32 + 32, :] = piece
    row = lax.broadcasted_iota(I32, (OWN, SEEDS), 0)
    for q in range(0, ND, 2):
        lanes = jnp.concatenate([send_ref[q : q + 1, :], send_ref[q + 1 : q + 2, :]], axis=1)
        hot = jnp.where(row == lanes, 1.0, 0.0).astype(BF)
        listed = dot(hot, hidden, 0, 0).astype(BF)
        for i in range(2):
            for h in range(2):
                piece = listed[i * SLOTS : (i + 1) * SLOTS, h * 128 : (h + 1) * 128]
                out_ref[q + i, h * SLOTS : (h + 1) * SLOTS, :] = piece
    hot = jnp.where(row == seed_ref[...], 1.0, 0.0).astype(BF)
    part_ref[...] = dot(dot(hot, hidden, 0, 0).astype(BF), w2s_ref[...])


def columns_body(chip_ref, rows_ref, *refs):
    keep_ref, give_ref = refs[NZ:]
    chip = chip_ref[0]
    total = jnp.zeros((2 * PAIR, HID), F32)
    for i, offset in enumerate(RING):
        source = jnp.bitwise_and(chip + offset, NZ - 1)
        total = total + dot(rows_ref[source], refs[i][...], 0, 0)
    keep_ref[0:COLS, :] = total[0:COLS]
    keep_ref[COLS:PAIR, :] = total[PAIR : PAIR + COLS]
    give_ref[0:COLS, :] = total[COLS:PAIR]
    give_ref[COLS:PAIR, :] = total[PAIR + COLS :]


def first_sum_body(in_ref, out_ref):
    total = in_ref[0, G2:, :].astype(F32)
    for p in range(1, ND):
        total = total + in_ref[p, G2:, :].astype(F32)
    total = total.astype(BF)
    for f in range(NF):
        out_ref[f] = total


def second_sum_body(two_ref, out_ref):
    two = two_ref[0].astype(F32)
    for f in range(1, NF):
        two = two + two_ref[f].astype(F32)
    two = two.astype(BF)
    for q in range(ND):
        out_ref[q] = two


def place_body(in_ref, g2s_ref, g2n_ref):
    for q in range(ND):
        g2 = g2s_ref if q < 8 else g2n_ref
        for h in range(2):
            piece = in_ref[q, h * 32 : h * 32 + 32, :].astype(F32)
            g2[(q % 8) * 32 : (q % 8) * 32 + 32, h * 128 : (h + 1) * 128] = piece


def layer_body(count_ref, neigh_ref, in_ref, part_ref, w2n_ref, layer_ref, hot):
    total = jnp.zeros((SEEDS, HID), F32)
    for s, picks in picks_by_source(count_ref, neigh_ref, hot):
        rows = [in_ref[s, 0:SLOTS, :], in_ref[s, SLOTS : 2 * SLOTS, :]]
        total = total + dot(picks, jnp.concatenate(rows, axis=1), 0, 0)
    mean_two = (total * (1.0 / K2)).astype(BF)
    layer_ref[...] = (part_ref[...] + dot(mean_two, w2n_ref[...])).astype(BF)


def swap(x, axis, groups=None):
    return lax.all_to_all(
        x, axis, split_axis=0, concat_axis=0, tiled=True, axis_index_groups=groups
    )


def turn(x, step):
    return lax.ppermute(x, "feat", [(i, (i + 2 * step) % NF) for i in range(NF)])


def along(x, step):
    pairs = [(i, (i + step) % ND if step % 4 == 0 else i // 4 * 4 + (i + step) % 4) for i in range(ND)]
    return lax.ppermute(x, "dom", pairs)


def fetch(x, bit):
    return lax.ppermute(x, "feat", [(i, i ^ bit) for i in range(NF)])


def per_device(
    features, w1_self, w1_neigh, w2_self, w2_neigh, neigh_one, send_rows, recv_count,
    neigh_two, seed_rows, d_out,
):
    f = lax.axis_index("feat")
    core = jnp.bitwise_and(f, 1).reshape(1)
    chip = jnp.right_shift(f, 1).reshape(1)
    chips = [[2 * z + c for z in range(NZ)] for c in range(2)]
    own = features[0]
    other = fetch(own, 1)
    ws_other = fetch(w1_self, 1)
    wn_other = fetch(w1_neigh, 1)

    send = send_rows[0, 0]
    seeds = seed_rows[0]
    grad_out = d_out[0, 0]
    counts = recv_count[:, 0, 0]
    names = neigh_two[0].transpose(2, 0, 1)
    hot = [pltpu.VMEM((K2, SLOTS, SEEDS), BF)]
    t_out = call(
        pick_body, "picks", shape((ND, SLOTS, HID), BF), [SMEM, VMEM, VMEM], hot, limit=60, us=4
    )(counts, names, grad_out)
    t_in = swap(t_out, "dom")

    rows = shape((NZ, OWN, 2 * PAIR), BF)
    rows, share = call(
        rows_body,
        "node_rows",
        (rows, rows),
        [SMEM, VMEM, VMEM, SMEM] + [VMEM] * 4,
        [pltpu.VMEM((NIN, PAIR), F32), pltpu.VMEM((HALF, PAIR), F32)],
        limit=60,
        us=22,
    )(core, own, other, neigh_one.reshape(-1), w1_self, w1_neigh, ws_other, wn_other)
    share = swap(share, "feat", chips)

    to_dom, part, d_pre = call(
        main_body,
        "project",
        (
            shape((ND, G2 + 64, 128), BF),
            shape((SEEDS, HID), F32),
            shape((OWN, HID), BF),
        ),
        [VMEM] * 7,
        us=4,
    )(share, t_in, send, seeds, grad_out, w2_self, w2_neigh)

    from_dom = swap(to_dom, "dom")
    ring = {0: d_pre}
    for i in range(1, 4):
        ring[-i], ring[i] = lax.optimization_barrier((turn(ring[1 - i], 1), turn(ring[i - 1], -1)))
    from_dom, last = lax.optimization_barrier((from_dom, ring[-3]))
    ring[-4] = turn(last, 1)
    two = call(first_sum_body, "sum_dom", shape((NF, 64, 128), BF), [VMEM])(from_dom)
    layer_out = call(
        layer_body,
        "layer_two",
        shape((SEEDS, HID), BF),
        [SMEM] + [VMEM] * 4,
        hot,
        us=5,
    )(counts, names, from_dom, part, w2_neigh)
    two, ring[-4], layer_out = lax.optimization_barrier((two, ring[-4], layer_out))
    two = swap(two, "feat")
    keep, give = call(
        columns_body,
        "columns",
        (shape((PAIR, HID), F32), shape((PAIR, HID), F32)),
        [SMEM] + [VMEM] * (1 + NZ),
        us=2,
    )(chip, rows, *[ring[i] for i in RING])
    one = keep + fetch(give, 1)
    one = one + sum(along(one, 4 * i) for i in range(1, 4))
    one, two = lax.optimization_barrier((one, two))
    one = one + sum(along(one, i) for i in range(1, 4))
    done = call(second_sum_body, "sum_feat", shape((ND, 64, 128), BF), [VMEM])(two)
    done = swap(done, "dom")
    second = shape((HID, HID), F32)
    two_self, two_neigh = call(place_body, "place", (second, second), [VMEM])(done)
    return (layer_out[None, None], one[:COLS], one[COLS:], two_self, two_neigh)


def solution(mesh):
    return jax.shard_map(
        per_device,
        mesh=mesh,
        in_specs=(
            P("dom", "feat", None),
            P("feat", None),
            P("feat", None),
            P(),
            P(),
            P("dom", None, None),
            P("dom", "feat", None, None),
            P(None, "feat", "dom"),
            P("dom", "feat", None, None),
            P("dom", "feat", None),
            P("dom", "feat", None, None),
        ),
        out_specs=(P("dom", "feat", None, None), P("feat", None), P("feat", None), P(), P()),
        check_vma=False,
    )
```

```python
import jax
import jax.numpy as jnp
from jax import lax
from jax.experimental import pallas as pl
from jax.experimental.pallas import tpu as pltpu
from jax.sharding import PartitionSpec as P

BF = jnp.bfloat16
F32 = jnp.float32
I32 = jnp.int32
NF = 16
ND = 16
NZ = 8
COLS = 64
PAIR = 128
NIN = 9216
R1 = 4608
OWN = 288
HALF = R1 // 2
K1 = 10
K2 = 15
SEEDS = 256
SLOTS = 128
HID = 256
UNROLL = 32
G2 = 256
RING = (0, -1, 1, -2, 2, -3, 3, -4)
VMEM = pl.BlockSpec(memory_space=pltpu.VMEM)
SMEM = pl.BlockSpec(memory_space=pltpu.SMEM)


def call(body, name, outs, ins, scratch=(), limit=16, us=1):
    return pl.pallas_call(
        body,
        name=name,
        out_shape=outs,
        in_specs=ins,
        out_specs=jax.tree.map(lambda _: VMEM, outs),
        scratch_shapes=list(scratch),
        compiler_params=pltpu.CompilerParams(vmem_limit_bytes=limit << 20),
        cost_estimate=pl.CostEstimate(flops=us * 10**9, transcendentals=0, bytes_accessed=us * 10**6),
    )


def shape(dims, dtype):
    return jax.ShapeDtypeStruct(dims, dtype)


def dot(a, b, ca=1, cb=0):
    return lax.dot_general(a, b, (((ca,), (cb,)), ((), ())), preferred_element_type=F32)


def picks_by_source(count_ref, neigh_ref, hot):
    names = neigh_ref[...].reshape(K2, SEEDS)
    source = jnp.zeros(names.shape, I32)
    base = jnp.zeros(names.shape, I32)
    start = jnp.int32(0)
    for s in range(1, ND):
        start = start + count_ref[s - 1]
        later = names >= start
        source = jnp.where(later, s, source)
        base = jnp.where(later, start, base)
    slot = names - base
    row = lax.broadcasted_iota(I32, (SLOTS, SEEDS), 0)
    for k in range(K2):
        hot[k] = jnp.where(row == slot[k : k + 1, :], 1.0, 0.0).astype(BF)
    for s in range(ND):
        here = jnp.where(source == s, 1.0, 0.0).astype(BF)
        total = jnp.zeros((SLOTS, SEEDS), BF)
        for k in range(K2):
            total = total + hot[k] * here[k : k + 1, :]
        yield s, total


def pick_body(count_ref, neigh_ref, dout_ref, t_ref, hot):
    d_out = dout_ref[...]
    for s, picks in picks_by_source(count_ref, neigh_ref, hot):
        t_ref[s] = dot(picks, d_out).astype(BF)


def rows_body(
    core_ref, own_ref, other_ref, index_ref, ws_ref, wn_ref, wso_ref, wno_ref,
    out_ref, part_ref, table, sums,
):
    core = core_ref[0]
    step = 512
    for c in range(0, NIN, step):
        both = jnp.concatenate([own_ref[:, c : c + step], other_ref[:, c : c + step]], axis=0)
        table[c : c + step, :] = both.astype(F32).T
    for z in range(NZ):
        first = pl.multiple_of((2 * z + core) * OWN, 32)
        out_ref[z, :, 0:PAIR] = table[pl.ds(first, OWN), :].astype(BF)

    def block(b, carry):
        z = b // (OWN // UNROLL)
        base = b * UNROLL + (z + core) * OWN
        for j in range(UNROLL):
            rows = [table[pl.ds(index_ref[k * R1 + base + j], 1), :] for k in range(K1)]
            while len(rows) > 1:
                even = len(rows) // 2 * 2
                rows = [rows[i] + rows[i + 1] for i in range(0, even, 2)] + rows[even:]
            sums[pl.ds(b * UNROLL + j, 1), :] = rows[0]
        return carry

    lax.fori_loop(0, HALF // UNROLL, block, 0)
    w = jnp.concatenate([ws_ref[...], wso_ref[...], wn_ref[...], wno_ref[...]], axis=0)
    for z in range(NZ):
        mean = sums[z * OWN : (z + 1) * OWN, :] * (1.0 / K1)
        out_ref[z, :, PAIR : 2 * PAIR] = mean.astype(BF)
        part_ref[z] = dot(out_ref[z], w).astype(BF)


def split(x):
    high = x.astype(BF)
    return high, (x - high.astype(F32)).astype(BF)


def owner_grads(in_ref, send_ref, seed_ref, dout_ref, w2s_ref, w2n_ref):
    row = lax.broadcasted_iota(I32, (OWN, SEEDS), 0)
    x = jnp.zeros((OWN, HID), F32)
    for q in range(0, ND, 2):
        lanes = jnp.concatenate([send_ref[q : q + 1, :], send_ref[q + 1 : q + 2, :]], axis=1)
        hot = jnp.where(row == lanes, 1.0, 0.0).astype(BF)
        x = x + dot(hot, in_ref[q : q + 2].reshape(2 * SLOTS, HID))
    x = x * (1.0 / K2)
    hot = jnp.where(row == seed_ref[...], 1.0, 0.0).astype(BF)
    d = dot(hot, dout_ref[...]).astype(BF)
    high, low = split(x)
    w2n = w2n_ref[...]
    d_hidden = dot(high, w2n, 1, 1) + dot(low, w2n, 1, 1) + dot(d, w2s_ref[...], 1, 1)
    return high, low, d, d_hidden


def hidden_body(
    share_ref, in_ref, send_ref, seed_ref, dout_ref, w2s_ref, w2n_ref,
    dpre_ref, hidden_ref, g2_ref,
):
    high, low, d, d_hidden = owner_grads(in_ref, send_ref, seed_ref, dout_ref, w2s_ref, w2n_ref)
    pre = share_ref[0].astype(F32)
    for z in range(1, NZ):
        pre = pre + share_ref[z].astype(F32)
    slope = jnp.exp(jnp.minimum(pre, 0.0))
    hidden = jnp.where(pre > 0, pre, slope - 1.0).astype(BF)
    dpre_ref[...] = (d_hidden * slope).astype(BF)
    hidden_ref[...] = hidden
    g2_ref[0:HID, :] = dot(hidden, d, 0, 0).astype(BF)
    g2_ref[HID:, :] = (dot(hidden, high, 0, 0) + dot(hidden, low, 0, 0)).astype(BF)


def outgoing_body(hidden_ref, g2_ref, send_ref, seed_ref, w2s_ref, out_ref, part_ref):
    hidden = hidden_ref[...]
    for q in range(ND):
        for h in range(2):
            piece = g2_ref[q * 32 : q * 32 + 32, h * 128 : (h + 1) * 128]
            out_ref[q, G2 + h * 32 : G2 + h * 32 + 32, :] = piece
    row = lax.broadcasted_iota(I32, (OWN, SEEDS), 0)
    for q in range(0, ND, 2):
        lanes = jnp.concatenate([send_ref[q : q + 1, :], send_ref[q + 1 : q + 2, :]], axis=1)
        hot = jnp.where(row == lanes, 1.0, 0.0).astype(BF)
        listed = dot(hot, hidden, 0, 0).astype(BF)
        for i in range(2):
            for h in range(2):
                piece = listed[i * SLOTS : (i + 1) * SLOTS, h * 128 : (h + 1) * 128]
                out_ref[q + i, h * SLOTS : (h + 1) * SLOTS, :] = piece
    hot = jnp.where(row == seed_ref[...], 1.0, 0.0).astype(BF)
    part_ref[...] = dot(dot(hot, hidden, 0, 0).astype(BF), w2s_ref[...])


def columns_body(chip_ref, rows_ref, *refs):
    keep_ref, give_ref = refs[NZ:]
    chip = chip_ref[0]
    total = jnp.zeros((2 * PAIR, HID), F32)
    for i, offset in enumerate(RING):
        source = jnp.bitwise_and(chip + offset, NZ - 1)
        total = total + dot(rows_ref[source], refs[i][...], 0, 0)
    keep_ref[0:COLS, :] = total[0:COLS]
    keep_ref[COLS:PAIR, :] = total[PAIR : PAIR + COLS]
    give_ref[0:COLS, :] = total[COLS:PAIR]
    give_ref[COLS:PAIR, :] = total[PAIR + COLS :]


def first_sum_body(in_ref, out_ref):
    total = in_ref[0, G2:, :].astype(F32)
    for p in range(1, ND):
        total = total + in_ref[p, G2:, :].astype(F32)
    total = total.astype(BF)
    for f in range(NF):
        out_ref[f] = total


def second_sum_body(two_ref, out_ref):
    two = two_ref[0].astype(F32)
    for f in range(1, NF):
        two = two + two_ref[f].astype(F32)
    two = two.astype(BF)
    for q in range(ND):
        out_ref[q] = two


def place_body(in_ref, g2s_ref, g2n_ref):
    for q in range(ND):
        g2 = g2s_ref if q < 8 else g2n_ref
        for h in range(2):
            piece = in_ref[q, h * 32 : h * 32 + 32, :].astype(F32)
            g2[(q % 8) * 32 : (q % 8) * 32 + 32, h * 128 : (h + 1) * 128] = piece


def layer_body(count_ref, neigh_ref, in_ref, part_ref, w2n_ref, layer_ref, hot):
    total = jnp.zeros((SEEDS, HID), F32)
    for s, picks in picks_by_source(count_ref, neigh_ref, hot):
        rows = [in_ref[s, 0:SLOTS, :], in_ref[s, SLOTS : 2 * SLOTS, :]]
        total = total + dot(picks, jnp.concatenate(rows, axis=1), 0, 0)
    mean_two = (total * (1.0 / K2)).astype(BF)
    layer_ref[...] = (part_ref[...] + dot(mean_two, w2n_ref[...])).astype(BF)


def swap(x, axis, groups=None):
    return lax.all_to_all(
        x, axis, split_axis=0, concat_axis=0, tiled=True, axis_index_groups=groups
    )


def turn(x, step):
    return lax.ppermute(x, "feat", [(i, (i + 2 * step) % NF) for i in range(NF)])


def along(x, step):
    pairs = [(i, (i + step) % ND if step % 4 == 0 else i // 4 * 4 + (i + step) % 4) for i in range(ND)]
    return lax.ppermute(x, "dom", pairs)


def fetch(x, bit):
    return lax.ppermute(x, "feat", [(i, i ^ bit) for i in range(NF)])


def per_device(
    features, w1_self, w1_neigh, w2_self, w2_neigh, neigh_one, send_rows, recv_count,
    neigh_two, seed_rows, d_out,
):
    f = lax.axis_index("feat")
    core = jnp.bitwise_and(f, 1).reshape(1)
    chip = jnp.right_shift(f, 1).reshape(1)
    chips = [[2 * z + c for z in range(NZ)] for c in range(2)]
    own = features[0]
    other = fetch(own, 1)
    ws_other = fetch(w1_self, 1)
    wn_other = fetch(w1_neigh, 1)

    send = send_rows[0, 0]
    seeds = seed_rows[0]
    grad_out = d_out[0, 0]
    counts = recv_count[:, 0, 0]
    names = neigh_two[0].transpose(2, 0, 1)
    hot = [pltpu.VMEM((K2, SLOTS, SEEDS), BF)]
    t_out = call(
        pick_body, "picks", shape((ND, SLOTS, HID), BF), [SMEM, VMEM, VMEM], hot, limit=60, us=4
    )(counts, names, grad_out)
    t_in = swap(t_out, "dom")

    rows = shape((NZ, OWN, 2 * PAIR), BF)
    rows, share = call(
        rows_body,
        "node_rows",
        (rows, rows),
        [SMEM, VMEM, VMEM, SMEM] + [VMEM] * 4,
        [pltpu.VMEM((NIN, PAIR), F32), pltpu.VMEM((HALF, PAIR), F32)],
        limit=60,
        us=22,
    )(core, own, other, neigh_one.reshape(-1), w1_self, w1_neigh, ws_other, wn_other)
    share = swap(share, "feat", chips)

    owned = shape((OWN, HID), BF)
    d_pre, hidden, g2 = call(
        hidden_body, "hidden", (owned, owned, shape((2 * HID, HID), BF)), [VMEM] * 7, us=2
    )(share, t_in, send, seeds, grad_out, w2_self, w2_neigh)

    to_dom, part = call(
        outgoing_body,
        "outgoing",
        (shape((ND, G2 + 64, 128), BF), shape((SEEDS, HID), F32)),
        [VMEM] * 5,
        us=2,
    )(hidden, g2, send, seeds, w2_self)
    ring = {0: d_pre}
    ring[-1], ring[1] = lax.optimization_barrier((turn(d_pre, 1), turn(d_pre, -1)))
    to_dom, ring[1] = lax.optimization_barrier((to_dom, ring[1]))
    from_dom = swap(to_dom, "dom")
    for i in range(2, 4):
        ring[-i], ring[i] = lax.optimization_barrier((turn(ring[1 - i], 1), turn(ring[i - 1], -1)))
    ring[-4] = turn(ring[-3], 1)
    from_dom, ring[-4] = lax.optimization_barrier((from_dom, ring[-4]))
    two = call(first_sum_body, "sum_dom", shape((NF, 64, 128), BF), [VMEM])(from_dom)
    layer_out = call(
        layer_body,
        "layer_two",
        shape((SEEDS, HID), BF),
        [SMEM] + [VMEM] * 4,
        hot,
        us=5,
    )(counts, names, from_dom, part, w2_neigh)
    two, ring[-4] = lax.optimization_barrier((two, ring[-4]))
    two = swap(two, "feat")
    keep, give = call(
        columns_body,
        "columns",
        (shape((PAIR, HID), F32), shape((PAIR, HID), F32)),
        [SMEM] + [VMEM] * (1 + NZ),
        us=2,
    )(chip, rows, *[ring[i] for i in RING])
    one = keep + fetch(give, 1)
    one = one + sum(along(one, 4 * i) for i in range(1, 4))
    one, two, layer_out = lax.optimization_barrier((one, two, layer_out))
    one = one + sum(along(one, i) for i in range(1, 4))
    done = call(second_sum_body, "sum_feat", shape((ND, 64, 128), BF), [VMEM])(two)
    done = swap(done, "dom")
    second = shape((HID, HID), F32)
    two_self, two_neigh = call(place_body, "place", (second, second), [VMEM])(done)
    return (layer_out[None, None], one[:COLS], one[COLS:], two_self, two_neigh)


def solution(mesh):
    return jax.shard_map(
        per_device,
        mesh=mesh,
        in_specs=(
            P("dom", "feat", None),
            P("feat", None),
            P("feat", None),
            P(),
            P(),
            P("dom", None, None),
            P("dom", "feat", None, None),
            P(None, "feat", "dom"),
            P("dom", "feat", None, None),
            P("dom", "feat", None),
            P("dom", "feat", None, None),
        ),
        out_specs=(P("dom", "feat", None, None), P("feat", None), P("feat", None), P(), P()),
        check_vma=False,
    )
```

```python
import jax
import jax.numpy as jnp
from jax import lax
from jax.experimental import pallas as pl
from jax.experimental.pallas import tpu as pltpu
from jax.sharding import PartitionSpec as P

BF = jnp.bfloat16
F32 = jnp.float32
I32 = jnp.int32
NF = 16
ND = 16
NZ = 8
COLS = 64
PAIR = 128
NIN = 9216
R1 = 4608
OWN = 288
HALF = R1 // 2
K1 = 10
K2 = 15
SEEDS = 256
SLOTS = 128
HID = 256
UNROLL = 32
G2 = 256
RING = (0, -1, 1, -2, 2, -3, 3, -4)
VMEM = pl.BlockSpec(memory_space=pltpu.VMEM)
SMEM = pl.BlockSpec(memory_space=pltpu.SMEM)


def call(body, name, outs, ins, scratch=(), limit=16, us=1):
    return pl.pallas_call(
        body,
        name=name,
        out_shape=outs,
        in_specs=ins,
        out_specs=jax.tree.map(lambda _: VMEM, outs),
        scratch_shapes=list(scratch),
        compiler_params=pltpu.CompilerParams(vmem_limit_bytes=limit << 20),
        cost_estimate=pl.CostEstimate(flops=us * 10**9, transcendentals=0, bytes_accessed=us * 10**6),
    )


def shape(dims, dtype):
    return jax.ShapeDtypeStruct(dims, dtype)


def dot(a, b, ca=1, cb=0):
    return lax.dot_general(a, b, (((ca,), (cb,)), ((), ())), preferred_element_type=F32)


def picks_by_source(count_ref, neigh_ref, hot):
    names = neigh_ref[...].reshape(K2, SEEDS)
    source = jnp.zeros(names.shape, I32)
    base = jnp.zeros(names.shape, I32)
    start = jnp.int32(0)
    for s in range(1, ND):
        start = start + count_ref[s - 1]
        later = names >= start
        source = jnp.where(later, s, source)
        base = jnp.where(later, start, base)
    slot = names - base
    row = lax.broadcasted_iota(I32, (SLOTS, SEEDS), 0)
    for k in range(K2):
        hot[k] = jnp.where(row == slot[k : k + 1, :], 1.0, 0.0).astype(BF)
    for s in range(ND):
        here = jnp.where(source == s, 1.0, 0.0).astype(BF)
        total = jnp.zeros((SLOTS, SEEDS), BF)
        for k in range(K2):
            total = total + hot[k] * here[k : k + 1, :]
        yield s, total


def pick_body(count_ref, neigh_ref, dout_ref, t_ref, hot):
    d_out = dout_ref[...]
    for s, picks in picks_by_source(count_ref, neigh_ref, hot):
        t_ref[s] = dot(picks, d_out).astype(BF)


def rows_body(
    core_ref, own_ref, other_ref, index_ref, ws_ref, wn_ref, wso_ref, wno_ref,
    out_ref, part_ref, table, sums,
):
    core = core_ref[0]
    step = 512
    for c in range(0, NIN, step):
        both = jnp.concatenate([own_ref[:, c : c + step], other_ref[:, c : c + step]], axis=0)
        table[c : c + step, :] = both.astype(F32).T
    for z in range(NZ):
        first = pl.multiple_of((2 * z + core) * OWN, 32)
        out_ref[z, :, 0:PAIR] = table[pl.ds(first, OWN), :].astype(BF)

    def block(b, carry):
        z = b // (OWN // UNROLL)
        base = b * UNROLL + (z + core) * OWN
        for j in range(UNROLL):
            rows = [table[pl.ds(index_ref[k * R1 + base + j], 1), :] for k in range(K1)]
            while len(rows) > 1:
                even = len(rows) // 2 * 2
                rows = [rows[i] + rows[i + 1] for i in range(0, even, 2)] + rows[even:]
            sums[pl.ds(b * UNROLL + j, 1), :] = rows[0]
        return carry

    lax.fori_loop(0, HALF // UNROLL, block, 0)
    w = jnp.concatenate([ws_ref[...], wso_ref[...], wn_ref[...], wno_ref[...]], axis=0)
    for z in range(NZ):
        mean = sums[z * OWN : (z + 1) * OWN, :] * (1.0 / K1)
        out_ref[z, :, PAIR : 2 * PAIR] = mean.astype(BF)
        part_ref[z] = dot(out_ref[z], w).astype(BF)


def split(x):
    high = x.astype(BF)
    return high, (x - high.astype(F32)).astype(BF)


def owner_grads(in_ref, send_ref, seed_ref, dout_ref, w2s_ref, w2n_ref):
    row = lax.broadcasted_iota(I32, (OWN, SEEDS), 0)
    x = jnp.zeros((OWN, HID), F32)
    for q in range(0, ND, 2):
        lanes = jnp.concatenate([send_ref[q : q + 1, :], send_ref[q + 1 : q + 2, :]], axis=1)
        hot = jnp.where(row == lanes, 1.0, 0.0).astype(BF)
        x = x + dot(hot, in_ref[q : q + 2].reshape(2 * SLOTS, HID))
    x = x * (1.0 / K2)
    hot = jnp.where(row == seed_ref[...], 1.0, 0.0).astype(BF)
    d = dot(hot, dout_ref[...]).astype(BF)
    high, low = split(x)
    w2n = w2n_ref[...]
    d_hidden = dot(high, w2n, 1, 1) + dot(low, w2n, 1, 1) + dot(d, w2s_ref[...], 1, 1)
    return high, low, d, d_hidden


def hidden_body(
    share_ref, in_ref, send_ref, seed_ref, dout_ref, w2s_ref, w2n_ref,
    dpre_ref, hidden_ref, g2_ref,
):
    high, low, d, d_hidden = owner_grads(in_ref, send_ref, seed_ref, dout_ref, w2s_ref, w2n_ref)
    pre = share_ref[0].astype(F32)
    for z in range(1, NZ):
        pre = pre + share_ref[z].astype(F32)
    slope = jnp.exp(jnp.minimum(pre, 0.0))
    hidden = jnp.where(pre > 0, pre, slope - 1.0).astype(BF)
    dpre_ref[...] = (d_hidden * slope).astype(BF)
    hidden_ref[...] = hidden
    g2_ref[0:HID, :] = dot(hidden, d, 0, 0).astype(BF)
    g2_ref[HID:, :] = (dot(hidden, high, 0, 0) + dot(hidden, low, 0, 0)).astype(BF)


def outgoing_body(hidden_ref, g2_ref, send_ref, seed_ref, w2s_ref, out_ref, part_ref):
    hidden = hidden_ref[...]
    for q in range(ND):
        for h in range(2):
            piece = g2_ref[q * 32 : q * 32 + 32, h * 128 : (h + 1) * 128]
            out_ref[q, G2 + h * 32 : G2 + h * 32 + 32, :] = piece
    row = lax.broadcasted_iota(I32, (OWN, SEEDS), 0)
    for q in range(0, ND, 2):
        lanes = jnp.concatenate([send_ref[q : q + 1, :], send_ref[q + 1 : q + 2, :]], axis=1)
        hot = jnp.where(row == lanes, 1.0, 0.0).astype(BF)
        listed = dot(hot, hidden, 0, 0).astype(BF)
        for i in range(2):
            for h in range(2):
                piece = listed[i * SLOTS : (i + 1) * SLOTS, h * 128 : (h + 1) * 128]
                out_ref[q + i, h * SLOTS : (h + 1) * SLOTS, :] = piece
    hot = jnp.where(row == seed_ref[...], 1.0, 0.0).astype(BF)
    part_ref[...] = dot(dot(hot, hidden, 0, 0).astype(BF), w2s_ref[...])


def columns_body(chip_ref, rows_ref, *refs):
    keep_ref, give_ref = refs[NZ:]
    chip = chip_ref[0]
    total = jnp.zeros((2 * PAIR, HID), F32)
    for i, offset in enumerate(RING):
        source = jnp.bitwise_and(chip + offset, NZ - 1)
        total = total + dot(rows_ref[source], refs[i][...], 0, 0)
    keep_ref[0:COLS, :] = total[0:COLS]
    keep_ref[COLS:PAIR, :] = total[PAIR : PAIR + COLS]
    give_ref[0:COLS, :] = total[COLS:PAIR]
    give_ref[COLS:PAIR, :] = total[PAIR + COLS :]


def first_sum_body(in_ref, out_ref):
    total = in_ref[0, G2:, :].astype(F32)
    for p in range(1, ND):
        total = total + in_ref[p, G2:, :].astype(F32)
    total = total.astype(BF)
    for f in range(NF):
        out_ref[f] = total


def second_sum_body(x_ref, two_ref, one_ref, out_ref):
    two = two_ref[0].astype(F32)
    for f in range(1, NF):
        two = two + two_ref[f].astype(F32)
    two = two.astype(BF)
    one = one_ref[pl.ds(pl.multiple_of(x_ref[0] * 32, 32), 32), :].astype(BF)
    for q in range(ND):
        out_ref[q, 0:64, :] = two
        for h in range(2):
            out_ref[q, 64 + h * 32 : 96 + h * 32, :] = one[:, h * 128 : (h + 1) * 128]


def place_body(in_ref, g1s_ref, g1n_ref, g2s_ref, g2n_ref):
    for h in range(2):
        lanes = slice(h * 128, (h + 1) * 128)
        for x in range(4):
            at = 64 + h * 32
            rows = in_ref[4 * x, at : at + 32, :].astype(F32)
            for y in range(1, 4):
                rows = rows + in_ref[4 * x + y, at : at + 32, :].astype(F32)
            g1 = g1s_ref if x < 2 else g1n_ref
            g1[x % 2 * 32 : x % 2 * 32 + 32, lanes] = rows
        for q in range(ND):
            g2 = g2s_ref if q < 8 else g2n_ref
            piece = in_ref[q, h * 32 : h * 32 + 32, :].astype(F32)
            g2[(q % 8) * 32 : (q % 8) * 32 + 32, lanes] = piece


def layer_body(count_ref, neigh_ref, in_ref, part_ref, w2n_ref, layer_ref, hot):
    total = jnp.zeros((SEEDS, HID), F32)
    for s, picks in picks_by_source(count_ref, neigh_ref, hot):
        rows = [in_ref[s, 0:SLOTS, :], in_ref[s, SLOTS : 2 * SLOTS, :]]
        total = total + dot(picks, jnp.concatenate(rows, axis=1), 0, 0)
    mean_two = (total * (1.0 / K2)).astype(BF)
    layer_ref[...] = (part_ref[...] + dot(mean_two, w2n_ref[...])).astype(BF)


def swap(x, axis, groups=None):
    return lax.all_to_all(
        x, axis, split_axis=0, concat_axis=0, tiled=True, axis_index_groups=groups
    )


def turn(x, step):
    return lax.ppermute(x, "feat", [(i, (i + 2 * step) % NF) for i in range(NF)])


def along_x(x, step):
    pairs = [(i, (i + 4 * step) % ND) for i in range(ND)]
    return lax.ppermute(x, "dom", pairs)


def fetch(x, bit):
    return lax.ppermute(x, "feat", [(i, i ^ bit) for i in range(NF)])


def per_device(
    features, w1_self, w1_neigh, w2_self, w2_neigh, neigh_one, send_rows, recv_count,
    neigh_two, seed_rows, d_out,
):
    f = lax.axis_index("feat")
    core = jnp.bitwise_and(f, 1).reshape(1)
    chip = jnp.right_shift(f, 1).reshape(1)
    chips = [[2 * z + c for z in range(NZ)] for c in range(2)]
    own = features[0]
    other = fetch(own, 1)
    ws_other = fetch(w1_self, 1)
    wn_other = fetch(w1_neigh, 1)

    send = send_rows[0, 0]
    seeds = seed_rows[0]
    grad_out = d_out[0, 0]
    counts = recv_count[:, 0, 0]
    names = neigh_two[0].transpose(2, 0, 1)
    hot = [pltpu.VMEM((K2, SLOTS, SEEDS), BF)]
    t_out = call(
        pick_body, "picks", shape((ND, SLOTS, HID), BF), [SMEM, VMEM, VMEM], hot, limit=60, us=4
    )(counts, names, grad_out)
    t_in = swap(t_out, "dom")

    rows = shape((NZ, OWN, 2 * PAIR), BF)
    rows, share = call(
        rows_body,
        "node_rows",
        (rows, rows),
        [SMEM, VMEM, VMEM, SMEM] + [VMEM] * 4,
        [pltpu.VMEM((NIN, PAIR), F32), pltpu.VMEM((HALF, PAIR), F32)],
        limit=60,
        us=22,
    )(core, own, other, neigh_one.reshape(-1), w1_self, w1_neigh, ws_other, wn_other)
    share = swap(share, "feat", chips)

    owned = shape((OWN, HID), BF)
    d_pre, hidden, g2 = call(
        hidden_body, "hidden", (owned, owned, shape((2 * HID, HID), BF)), [VMEM] * 7, us=2
    )(share, t_in, send, seeds, grad_out, w2_self, w2_neigh)

    to_dom, part = call(
        outgoing_body,
        "outgoing",
        (shape((ND, G2 + 64, 128), BF), shape((SEEDS, HID), F32)),
        [VMEM] * 5,
        us=2,
    )(hidden, g2, send, seeds, w2_self)
    ring = {0: d_pre}
    ring[-1], ring[1] = lax.optimization_barrier((turn(d_pre, 1), turn(d_pre, -1)))
    to_dom, ring[1] = lax.optimization_barrier((to_dom, ring[1]))
    from_dom = swap(to_dom, "dom")
    for i in range(2, 4):
        ring[-i], ring[i] = lax.optimization_barrier((turn(ring[1 - i], 1), turn(ring[i - 1], -1)))
    ring[-4] = turn(ring[-3], 1)
    from_dom, ring[-4] = lax.optimization_barrier((from_dom, ring[-4]))
    two = call(first_sum_body, "sum_dom", shape((NF, 64, 128), BF), [VMEM])(from_dom)
    layer_out = call(
        layer_body,
        "layer_two",
        shape((SEEDS, HID), BF),
        [SMEM] + [VMEM] * 4,
        hot,
        us=5,
    )(counts, names, from_dom, part, w2_neigh)
    two, ring[-4] = lax.optimization_barrier((two, ring[-4]))
    two = swap(two, "feat")
    keep, give = call(
        columns_body,
        "columns",
        (shape((PAIR, HID), F32), shape((PAIR, HID), F32)),
        [SMEM] + [VMEM] * (1 + NZ),
        us=2,
    )(chip, rows, *[ring[i] for i in RING])
    one = keep + fetch(give, 1)
    one = one + sum(along_x(one, i) for i in range(1, 4))
    one, two, layer_out = lax.optimization_barrier((one, two, layer_out))
    x = jnp.right_shift(lax.axis_index("dom"), 2).reshape(1)
    done = call(
        second_sum_body, "sum_feat", shape((ND, 128, 128), BF), [SMEM] + [VMEM] * 2
    )(x, two, one)
    done = swap(done, "dom")
    first = shape((COLS, HID), F32)
    second = shape((HID, HID), F32)
    grads = call(place_body, "place", (first, first, second, second), [VMEM])(done)
    return (layer_out[None, None], *grads)


def solution(mesh):
    return jax.shard_map(
        per_device,
        mesh=mesh,
        in_specs=(
            P("dom", "feat", None),
            P("feat", None),
            P("feat", None),
            P(),
            P(),
            P("dom", None, None),
            P("dom", "feat", None, None),
            P(None, "feat", "dom"),
            P("dom", "feat", None, None),
            P("dom", "feat", None),
            P("dom", "feat", None, None),
        ),
        out_specs=(P("dom", "feat", None, None), P("feat", None), P("feat", None), P(), P()),
        check_vma=False,
    )
```

```python
import jax
import jax.numpy as jnp
from jax import lax
from jax.experimental import pallas as pl
from jax.experimental.pallas import tpu as pltpu
from jax.sharding import PartitionSpec as P

BF = jnp.bfloat16
F32 = jnp.float32
I32 = jnp.int32
NF = 16
ND = 16
NZ = 8
COLS = 64
PAIR = 128
NIN = 9216
R1 = 4608
OWN = 288
HALF = R1 // 2
K1 = 10
K2 = 15
SEEDS = 256
SLOTS = 128
HID = 256
UNROLL = 32
G2 = 256
RING = (0, -1, 1, -2, 2, -3, 3, -4)
VMEM = pl.BlockSpec(memory_space=pltpu.VMEM)
SMEM = pl.BlockSpec(memory_space=pltpu.SMEM)


def call(body, name, outs, ins, scratch=(), limit=16, us=1):
    return pl.pallas_call(
        body,
        name=name,
        out_shape=outs,
        in_specs=ins,
        out_specs=jax.tree.map(lambda _: VMEM, outs),
        scratch_shapes=list(scratch),
        compiler_params=pltpu.CompilerParams(vmem_limit_bytes=limit << 20),
        cost_estimate=pl.CostEstimate(flops=us * 10**9, transcendentals=0, bytes_accessed=us * 10**6),
    )


def shape(dims, dtype):
    return jax.ShapeDtypeStruct(dims, dtype)


def dot(a, b, ca=1, cb=0):
    return lax.dot_general(a, b, (((ca,), (cb,)), ((), ())), preferred_element_type=F32)


def picks_by_source(count_ref, neigh_ref, hot):
    names = neigh_ref[...].reshape(K2, SEEDS)
    source = jnp.zeros(names.shape, I32)
    base = jnp.zeros(names.shape, I32)
    start = jnp.int32(0)
    for s in range(1, ND):
        start = start + count_ref[s - 1]
        later = names >= start
        source = jnp.where(later, s, source)
        base = jnp.where(later, start, base)
    slot = names - base
    row = lax.broadcasted_iota(I32, (SLOTS, SEEDS), 0)
    for k in range(K2):
        hot[k] = jnp.where(row == slot[k : k + 1, :], 1.0, 0.0).astype(BF)
    for s in range(ND):
        here = jnp.where(source == s, 1.0, 0.0).astype(BF)
        total = jnp.zeros((SLOTS, SEEDS), BF)
        for k in range(K2):
            total = total + hot[k] * here[k : k + 1, :]
        yield s, total


def pick_body(count_ref, neigh_ref, dout_ref, t_ref, hot):
    d_out = dout_ref[...]
    for s, picks in picks_by_source(count_ref, neigh_ref, hot):
        t_ref[s] = dot(picks, d_out).astype(BF)


def rows_body(
    core_ref, own_ref, other_ref, index_ref, ws_ref, wn_ref, wso_ref, wno_ref,
    out_ref, part_ref, table, sums,
):
    core = core_ref[0]
    step = 512
    for c in range(0, NIN, step):
        both = jnp.concatenate([own_ref[:, c : c + step], other_ref[:, c : c + step]], axis=0)
        table[c : c + step, :] = both.astype(F32).T
    for z in range(NZ):
        first = pl.multiple_of((2 * z + core) * OWN, 32)
        out_ref[z, :, 0:PAIR] = table[pl.ds(first, OWN), :].astype(BF)

    def block(b, carry):
        z = b // (OWN // UNROLL)
        base = b * UNROLL + (z + core) * OWN
        for j in range(UNROLL):
            rows = [table[pl.ds(index_ref[k * R1 + base + j], 1), :] for k in range(K1)]
            while len(rows) > 1:
                even = len(rows) // 2 * 2
                rows = [rows[i] + rows[i + 1] for i in range(0, even, 2)] + rows[even:]
            sums[pl.ds(b * UNROLL + j, 1), :] = rows[0]
        return carry

    lax.fori_loop(0, HALF // UNROLL, block, 0)
    w = jnp.concatenate([ws_ref[...], wso_ref[...], wn_ref[...], wno_ref[...]], axis=0)
    for z in range(NZ):
        mean = sums[z * OWN : (z + 1) * OWN, :] * (1.0 / K1)
        out_ref[z, :, PAIR : 2 * PAIR] = mean.astype(BF)
        part_ref[z] = dot(out_ref[z], w).astype(BF)


def split(x):
    high = x.astype(BF)
    return high, (x - high.astype(F32)).astype(BF)


def owner_grads(in_ref, send_ref, seed_ref, dout_ref, w2s_ref, w2n_ref):
    row = lax.broadcasted_iota(I32, (OWN, SEEDS), 0)
    x = jnp.zeros((OWN, HID), F32)
    for q in range(0, ND, 2):
        lanes = jnp.concatenate([send_ref[q : q + 1, :], send_ref[q + 1 : q + 2, :]], axis=1)
        hot = jnp.where(row == lanes, 1.0, 0.0).astype(BF)
        x = x + dot(hot, in_ref[q : q + 2].reshape(2 * SLOTS, HID))
    x = x * (1.0 / K2)
    hot = jnp.where(row == seed_ref[...], 1.0, 0.0).astype(BF)
    d = dot(hot, dout_ref[...]).astype(BF)
    high, low = split(x)
    w2n = w2n_ref[...]
    d_hidden = dot(high, w2n, 1, 1) + dot(low, w2n, 1, 1) + dot(d, w2s_ref[...], 1, 1)
    return high, low, d, d_hidden


def hidden_body(
    share_ref, in_ref, send_ref, seed_ref, dout_ref, w2s_ref, w2n_ref,
    dpre_ref, hidden_ref, g2_ref,
):
    high, low, d, d_hidden = owner_grads(in_ref, send_ref, seed_ref, dout_ref, w2s_ref, w2n_ref)
    pre = share_ref[0].astype(F32)
    for z in range(1, NZ):
        pre = pre + share_ref[z].astype(F32)
    slope = jnp.exp(jnp.minimum(pre, 0.0))
    hidden = jnp.where(pre > 0, pre, slope - 1.0).astype(BF)
    dpre_ref[...] = (d_hidden * slope).astype(BF)
    hidden_ref[...] = hidden
    g2_ref[0:HID, :] = dot(hidden, d, 0, 0).astype(BF)
    g2_ref[HID:, :] = (dot(hidden, high, 0, 0) + dot(hidden, low, 0, 0)).astype(BF)


def outgoing_body(hidden_ref, g2_ref, send_ref, seed_ref, w2s_ref, out_ref, part_ref):
    hidden = hidden_ref[...]
    for q in range(ND):
        for h in range(2):
            piece = g2_ref[q * 32 : q * 32 + 32, h * 128 : (h + 1) * 128]
            out_ref[q, G2 + h * 32 : G2 + h * 32 + 32, :] = piece
    row = lax.broadcasted_iota(I32, (OWN, SEEDS), 0)
    for q in range(0, ND, 2):
        lanes = jnp.concatenate([send_ref[q : q + 1, :], send_ref[q + 1 : q + 2, :]], axis=1)
        hot = jnp.where(row == lanes, 1.0, 0.0).astype(BF)
        listed = dot(hot, hidden, 0, 0).astype(BF)
        for i in range(2):
            for h in range(2):
                piece = listed[i * SLOTS : (i + 1) * SLOTS, h * 128 : (h + 1) * 128]
                out_ref[q + i, h * SLOTS : (h + 1) * SLOTS, :] = piece
    hot = jnp.where(row == seed_ref[...], 1.0, 0.0).astype(BF)
    part_ref[...] = dot(dot(hot, hidden, 0, 0).astype(BF), w2s_ref[...])


def columns_body(chip_ref, rows_ref, *refs):
    keep_ref, give_ref = refs[NZ:]
    chip = chip_ref[0]
    total = jnp.zeros((2 * PAIR, HID), F32)
    for i, offset in enumerate(RING):
        source = jnp.bitwise_and(chip + offset, NZ - 1)
        total = total + dot(rows_ref[source], refs[i][...], 0, 0)
    keep_ref[0:COLS, :] = total[0:COLS]
    keep_ref[COLS:PAIR, :] = total[PAIR : PAIR + COLS]
    give_ref[0:COLS, :] = total[COLS:PAIR]
    give_ref[COLS:PAIR, :] = total[PAIR + COLS :]


def first_sum_body(in_ref, out_ref):
    total = in_ref[0, G2:, :].astype(F32)
    for p in range(1, ND):
        total = total + in_ref[p, G2:, :].astype(F32)
    total = total.astype(BF)
    for f in range(NF):
        out_ref[f] = total


def second_sum_body(x_ref, two_ref, one_ref, out_ref):
    two = two_ref[0].astype(F32)
    for f in range(1, NF):
        two = two + two_ref[f].astype(F32)
    two = two.astype(BF)
    one = one_ref[pl.ds(pl.multiple_of(x_ref[0] * 32, 32), 32), :].astype(BF)
    for q in range(ND):
        out_ref[q, 0:64, :] = two
        for h in range(2):
            out_ref[q, 64 + h * 32 : 96 + h * 32, :] = one[:, h * 128 : (h + 1) * 128]


def place_body(in_ref, g1s_ref, g1n_ref, g2s_ref, g2n_ref):
    for h in range(2):
        lanes = slice(h * 128, (h + 1) * 128)
        for x in range(4):
            at = 64 + h * 32
            rows = in_ref[4 * x, at : at + 32, :].astype(F32)
            for y in range(1, 4):
                rows = rows + in_ref[4 * x + y, at : at + 32, :].astype(F32)
            g1 = g1s_ref if x < 2 else g1n_ref
            g1[x % 2 * 32 : x % 2 * 32 + 32, lanes] = rows
        for q in range(ND):
            g2 = g2s_ref if q < 8 else g2n_ref
            piece = in_ref[q, h * 32 : h * 32 + 32, :].astype(F32)
            g2[(q % 8) * 32 : (q % 8) * 32 + 32, lanes] = piece


def layer_body(count_ref, neigh_ref, in_ref, part_ref, w2n_ref, layer_ref, hot):
    total = jnp.zeros((SEEDS, HID), F32)
    for s, picks in picks_by_source(count_ref, neigh_ref, hot):
        rows = [in_ref[s, 0:SLOTS, :], in_ref[s, SLOTS : 2 * SLOTS, :]]
        total = total + dot(picks, jnp.concatenate(rows, axis=1), 0, 0)
    mean_two = (total * (1.0 / K2)).astype(BF)
    layer_ref[...] = (part_ref[...] + dot(mean_two, w2n_ref[...])).astype(BF)


def swap(x, axis, groups=None):
    return lax.all_to_all(
        x, axis, split_axis=0, concat_axis=0, tiled=True, axis_index_groups=groups
    )


def turn(x, step):
    return lax.ppermute(x, "feat", [(i, (i + 2 * step) % NF) for i in range(NF)])


def along_x(x, step):
    pairs = [(i, (i + 4 * step) % ND) for i in range(ND)]
    return lax.ppermute(x, "dom", pairs)


def fetch(x, bit):
    return lax.ppermute(x, "feat", [(i, i ^ bit) for i in range(NF)])


def per_device(
    features, w1_self, w1_neigh, w2_self, w2_neigh, neigh_one, send_rows, recv_count,
    neigh_two, seed_rows, d_out,
):
    f = lax.axis_index("feat")
    core = jnp.bitwise_and(f, 1).reshape(1)
    chip = jnp.right_shift(f, 1).reshape(1)
    chips = [[2 * z + c for z in range(NZ)] for c in range(2)]
    own = features[0]
    other = fetch(own, 1)
    ws_other = fetch(w1_self, 1)
    wn_other = fetch(w1_neigh, 1)

    send = send_rows[0, 0]
    seeds = seed_rows[0]
    grad_out = d_out[0, 0]
    counts = recv_count[:, 0, 0]
    names = neigh_two[0].transpose(2, 0, 1)
    hot = [pltpu.VMEM((K2, SLOTS, SEEDS), BF)]
    t_out = call(
        pick_body, "picks", shape((ND, SLOTS, HID), BF), [SMEM, VMEM, VMEM], hot, limit=60, us=4
    )(counts, names, grad_out)
    t_in = swap(t_out, "dom")

    rows = shape((NZ, OWN, 2 * PAIR), BF)
    rows, share = call(
        rows_body,
        "node_rows",
        (rows, rows),
        [SMEM, VMEM, VMEM, SMEM] + [VMEM] * 4,
        [pltpu.VMEM((NIN, PAIR), F32), pltpu.VMEM((HALF, PAIR), F32)],
        limit=60,
        us=22,
    )(core, own, other, neigh_one.reshape(-1), w1_self, w1_neigh, ws_other, wn_other)
    share = swap(share, "feat", chips)

    owned = shape((OWN, HID), BF)
    d_pre, hidden, g2 = call(
        hidden_body, "hidden", (owned, owned, shape((2 * HID, HID), BF)), [VMEM] * 7, us=2
    )(share, t_in, send, seeds, grad_out, w2_self, w2_neigh)

    to_dom, part = call(
        outgoing_body,
        "outgoing",
        (shape((ND, G2 + 64, 128), BF), shape((SEEDS, HID), F32)),
        [VMEM] * 5,
        us=2,
    )(hidden, g2, send, seeds, w2_self)
    ring = {0: d_pre}
    ring[-1], ring[1] = lax.optimization_barrier((turn(d_pre, 1), turn(d_pre, -1)))
    to_dom, ring[1] = lax.optimization_barrier((to_dom, ring[1]))
    from_dom = swap(to_dom, "dom")
    for i in range(2, 4):
        ring[-i], ring[i] = lax.optimization_barrier((turn(ring[1 - i], 1), turn(ring[i - 1], -1)))
    ring[-4] = turn(ring[-3], 1)
    from_dom, ring[-4] = lax.optimization_barrier((from_dom, ring[-4]))
    two = call(first_sum_body, "sum_dom", shape((NF, 64, 128), BF), [VMEM])(from_dom)
    layer_out = call(
        layer_body,
        "layer_two",
        shape((SEEDS, HID), BF),
        [SMEM] + [VMEM] * 4,
        hot,
        us=5,
    )(counts, names, from_dom, part, w2_neigh)
    two, ring[-4] = lax.optimization_barrier((two, ring[-4]))
    two = swap(two, "feat")
    keep, give = call(
        columns_body,
        "columns",
        (shape((PAIR, HID), F32), shape((PAIR, HID), F32)),
        [SMEM] + [VMEM] * (1 + NZ),
        us=2,
    )(chip, rows, *[ring[i] for i in RING])
    one = keep + fetch(give, 1)
    rounded = one.astype(BF)
    one = one + sum(along_x(rounded, i).astype(F32) for i in range(1, 4))
    one, two, layer_out = lax.optimization_barrier((one, two, layer_out))
    x = jnp.right_shift(lax.axis_index("dom"), 2).reshape(1)
    done = call(
        second_sum_body, "sum_feat", shape((ND, 128, 128), BF), [SMEM] + [VMEM] * 2
    )(x, two, one)
    done = swap(done, "dom")
    first = shape((COLS, HID), F32)
    second = shape((HID, HID), F32)
    grads = call(place_body, "place", (first, first, second, second), [VMEM])(done)
    return (layer_out[None, None], *grads)


def solution(mesh):
    return jax.shard_map(
        per_device,
        mesh=mesh,
        in_specs=(
            P("dom", "feat", None),
            P("feat", None),
            P("feat", None),
            P(),
            P(),
            P("dom", None, None),
            P("dom", "feat", None, None),
            P(None, "feat", "dom"),
            P("dom", "feat", None, None),
            P("dom", "feat", None),
            P("dom", "feat", None, None),
        ),
        out_specs=(P("dom", "feat", None, None), P("feat", None), P("feat", None), P(), P()),
        check_vma=False,
    )
```
